32 devices in a mesh: groups: 2 (over y), section: 4 (over z), tp: 2 (over core), sp: 2 (over x).
Axes of the slice: x: 2, y: 2, z: 4, core: 2. Of those that a mesh axis runs over, the one named last changes fastest.
Arguments:
- hidden: bfloat16 [1024, 6144], P(('groups', 'sp', 'section'), 'tp'), parts along dimension 0, may hold values from -6 to 6
- modulation: float32 [2, 6144], P(None, 'tp'), may hold values from -2 to 2
- time_embed: float32 [12288], P(('groups', 'tp')), parts along dimension 0, may hold values from -2 to 2
- head_weight: bfloat16 [6144, 64], P('tp'), may hold values from -0.078125 to 0.078125
- head_bias: float32 [64], replicated, may hold values from -2 to 2
- noisy: bfloat16 [16, 16, 16, 16], P(('groups', 'sp'), None, 'section'), parts along dimension 0, may hold values from -6 to 6
- step_size: float32 [2], P('groups'), parts along dimension 0, may hold values from 0.2 to 0.6
- latent_mean: float32 [16], replicated, may hold values from -2 to 2
- latent_std: float32 [16], replicated, may hold values from 0.5 to 2
- in_weight: bfloat16 [27, 16, 512], P(None, None, 'tp'), may hold values from -0.3125 to 0.3125
- in_bias: float32 [512], P('tp'), may hold values from -2 to 2
- norm_gain: float32 [512], replicated, may hold values from 0.25 to 1.75
- conv_weight: bfloat16 [27, 512, 512], P(None, 'section', 'tp'), may hold values from -0.0546875 to 0.0546875
- conv_bias: float32 [512], P('tp'), may hold values from -2 to 2
Outputs:
- decoded: bfloat16 [16, 16, 16, 512], P(('groups', 'sp'), None, 'section', 'tp'), parts along dimension 0
The draws below stay inside these ranges and needn't reach their ends.
There are 2 independent parts, one for each index of `groups`. The reference program is written for one: setup_inputs(seed, part) draws one part's arguments, and reference() takes and returns one part's arrays. A program takes and returns all parts, laid end to end along the dimension named above; an argument that names none is the same for every part. Nothing has to cross between parts.
All inputs are finite; a program needn't handle non-finite values.
Results may differ from the reference program's by a relative error of at most 0.006.
Values may be sent and summed in bfloat16 or wider, within the bound.
No kernel may reach another device: no remote copies, remote signals or barrier semaphores. Data moves between devices by JAX's collectives and lax.ppermute only.
A program may use at most 128 MiB of HBM per device.

```python
import math
import jax
import jax.numpy as jnp
from jax import lax

D = 6144
LAT_CH = 16
CH = 512
HEIGHT = 16
PCH = 64
FRAMES = 8
WIDTH = 16
TOKENS = 512


def block_scale(own_key, dims, shards, low, high):
    gain = 1.0
    for dim, blocks in shards:
        steps = jax.random.uniform(jax.random.fold_in(jax.random.fold_in(own_key, 6), dim), (blocks,), jnp.float32, low / len(shards), high / len(shards))
        gain = gain * jnp.repeat(jnp.exp(steps), dims[dim] // blocks).reshape((-1,) + (1,) * (len(dims) - 1 - dim))
    return gain


def gaussian(stream_key, dims, scale, bound, cuts=(), dtype=jnp.bfloat16):
    values = scale * jax.random.normal(stream_key, dims, jnp.float32)
    if cuts:
        values = values * block_scale(stream_key, dims, cuts, -0.22, 0.18)
    return jnp.clip(values, -bound, bound).astype(dtype)


def setup_inputs(seed: int = 0, part: int = 0) -> dict:
    arg_keys = jax.random.split(jax.random.key(seed), 15)
    part_splits = jax.random.split(jax.random.fold_in(arg_keys[14], part), 15)
    return {
        "hidden": gaussian(part_splits[0], (TOKENS, D), 1.0, 6.0, ((0, 8), (1, 2))),
        "modulation": gaussian(arg_keys[1], (2, D), 0.3, 2.0, ((1, 2),), jnp.float32),
        "time_embed": gaussian(part_splits[2], (D,), 0.3, 2.0, ((0, 2),), jnp.float32),
        "head_weight": gaussian(arg_keys[3], (D, PCH), D ** -0.5, 0.078125, ((0, 2),)),
        "head_bias": gaussian(arg_keys[4], (PCH,), 0.3, 2.0, (), jnp.float32),
        "noisy": gaussian(part_splits[5], (FRAMES, HEIGHT, WIDTH, LAT_CH), 1.0, 6.0, ((0, 2), (2, 4))),
        "step_size": jnp.clip(jax.random.uniform(part_splits[6], (1,), jnp.float32, 0.2, 0.6), 0.2, 0.6),
        "latent_mean": gaussian(arg_keys[7], (LAT_CH,), 0.5, 2.0, (), jnp.float32),
        "latent_std": jnp.clip(jnp.exp(jax.random.uniform(arg_keys[8], (LAT_CH,), jnp.float32, math.log(0.5), math.log(2.0))), 0.5, 2.0),
        "in_weight": gaussian(arg_keys[9], (27, LAT_CH, CH), (27 * LAT_CH) ** -0.5, 0.3125, ((2, 2),)),
        "in_bias": gaussian(arg_keys[10], (CH,), 0.3, 2.0, ((0, 2),), jnp.float32),
        "norm_gain": jnp.clip(1.0 + 0.15 * jax.random.normal(arg_keys[11], (CH,), jnp.float32), 0.25, 1.75),
        "conv_weight": gaussian(arg_keys[12], (27, CH, CH), (27 * CH) ** -0.5, 0.0546875, ((1, 4), (2, 2))),
        "conv_bias": gaussian(arg_keys[13], (CH,), 0.3, 2.0, ((0, 2),), jnp.float32),
    }


def conv_taps(padded, weight, frames, height, columns):
    channels = padded.shape[3]
    result = jnp.zeros((frames * height * columns, weight.shape[2]), jnp.float32)
    for offset_time in range(3):
        for offset_row in range(3):
            for offset_col in range(3):
                window = padded[offset_time:offset_time + frames, offset_row:offset_row + height, offset_col:offset_col + columns]
                result = result + jnp.dot(window.reshape(-1, channels), weight[9 * offset_time + 3 * offset_row + offset_col], preferred_element_type=jnp.float32)
    return result

def activate(source, gain_vector):
    values = source.astype(jnp.float32)
    squares = lax.optimization_barrier(jnp.mean(values * values, axis=-1, keepdims=True))
    return jax.nn.silu(values * lax.rsqrt(squares + 1e-06) * gain_vector).astype(jnp.bfloat16)

def reference(hidden, modulation, time_embed, head_weight, head_bias, noisy, step_size, latent_mean, latent_std, in_weight, in_bias, norm_gain, conv_weight, conv_bias):
    values = hidden.astype(jnp.float32)
    average = lax.optimization_barrier(jnp.sum(values, axis=1)) / D
    variance = lax.optimization_barrier(jnp.sum(values * values, axis=1)) / D - average * average
    shift_term = modulation[0] + time_embed
    scale_term = modulation[1] + time_embed
    modulated = ((values - average[:, None]) * lax.rsqrt(variance[:, None] + 1e-06) * (1.0 + scale_term) + shift_term).astype(jnp.bfloat16)
    velocity = (jnp.dot(modulated, head_weight, preferred_element_type=jnp.float32) + head_bias).astype(jnp.bfloat16)
    latent_field = velocity.reshape(FRAMES, HEIGHT // 2, WIDTH // 2, 2, 2, LAT_CH)
    latent_field = jnp.transpose(latent_field, (0, 1, 3, 2, 4, 5)).reshape(FRAMES, HEIGHT, WIDTH, LAT_CH)
    latent = ((noisy.astype(jnp.float32) - step_size[0] * latent_field.astype(jnp.float32)) * latent_std + latent_mean).astype(jnp.bfloat16)
    padded = jnp.pad(latent, ((2, 0), (1, 1), (1, 1), (0, 0)))
    upblock = (conv_taps(padded, in_weight, FRAMES, HEIGHT, WIDTH) + in_bias).astype(jnp.bfloat16)
    normed = activate(upblock, norm_gain).reshape(FRAMES, HEIGHT, WIDTH, CH)
    conv_input = jnp.pad(normed, ((2, 0), (1, 1), (1, 1), (0, 0)))
    mixed = conv_taps(conv_input, conv_weight, FRAMES, HEIGHT, WIDTH)
    decoded = (upblock.astype(jnp.float32) + mixed + conv_bias).astype(jnp.bfloat16)
    return decoded.reshape(FRAMES, HEIGHT, WIDTH, CH)
```

```python
import jax
import jax.numpy as jnp
import numpy as np
from jax import lax
from jax.experimental import pallas as pl
from jax.experimental.pallas import tpu as pltpu
from jax.sharding import PartitionSpec as P

F32 = jnp.float32
BF16 = jnp.bfloat16


def padded_2(value, sides, width):
    for axis, dim in sides:
        count, length = (lax.axis_size(axis), value.shape[dim])
        up = [(i, (i + 1) % count) for i in range(count - 1)]
        down = [(j, i) for i, j in up]
        last = lax.slice_in_dim(value, length - width, length, axis=dim)
        leading = lax.slice_in_dim(value, 0, width, axis=dim)
        before = lax.ppermute(last, axis, up)
        after = lax.ppermute(leading, axis, down)
        value = jnp.concatenate([before, value, after], axis=dim)
    return value


def passed_along(value, axis, by):
    count = lax.axis_size(axis)
    pairs = [(i, i + by) for i in range(count) if 0 <= i + by < count]
    return lax.ppermute(value, axis, pairs)


def conv_taps(padded, weight, frames, height, columns):
    channels = padded.shape[3]
    result = jnp.zeros((frames * height * columns, weight.shape[2]), jnp.float32)
    for offset_time in range(3):
        for offset_row in range(3):
            slab = padded[offset_time : offset_time + frames, offset_row : offset_row + height]
            window = jnp.concatenate(
                [slab[:, :, 0:columns], slab[:, :, 1 : columns + 1], slab[:, :, 2 : columns + 2]],
                axis=3,
            )
            first = 9 * offset_time + 3 * offset_row
            taps = weight[first : first + 3].reshape(3 * channels, weight.shape[2])
            result = result + jnp.dot(
                window.reshape(-1, 3 * channels), taps, preferred_element_type=jnp.float32
            )
    return result


def activate(source, gain_vector):
    values = source.astype(jnp.float32)
    squares = jnp.mean(values * values, axis=-1, keepdims=True)
    return jax.nn.silu(values * lax.rsqrt(squares + 1e-06) * gain_vector).astype(jnp.bfloat16)


def pad_rows(source):
    return jnp.pad(source, ((0, 0), (1, 1), (0, 0), (0, 0)))


def general_shards(
    hidden, modulation, time_embed, head_weight, head_bias, noisy, step_size,
    latent_mean, latent_std, in_weight, in_bias, norm_gain, conv_weight, conv_bias,
):
    frames, height, columns, lat_channels = noisy.shape
    sections = lax.axis_size("section")
    half_channels = in_weight.shape[2]
    features = hidden.shape[1] * lax.axis_size("tp")
    values = hidden.astype(jnp.float32)
    row_sums, square_sums = lax.psum(
        (jnp.sum(values, axis=1), jnp.sum(values * values, axis=1)), "tp"
    )
    average = row_sums / features
    variance = square_sums / features - average * average
    shift_term = modulation[0] + time_embed
    scale_term = modulation[1] + time_embed
    modulated = (
        (values - average[:, None]) * lax.rsqrt(variance[:, None] + 1e-06) * (1.0 + scale_term)
        + shift_term
    ).astype(jnp.bfloat16)
    partial_sum = jnp.dot(modulated, head_weight, preferred_element_type=jnp.float32)
    velocity = (lax.psum(partial_sum, "tp") + head_bias).astype(jnp.bfloat16)
    band_rows = velocity.shape[0] * 2 // (columns * sections)
    outgoing = velocity.reshape(band_rows, sections, -1)
    arrived = lax.all_to_all(outgoing, "section", split_axis=1, concat_axis=0, tiled=True)
    latent_field = arrived.reshape(frames, height // 2, columns // 2, 2, 2, lat_channels)
    latent_field = jnp.transpose(latent_field, (0, 1, 3, 2, 4, 5)).reshape(
        frames, height, columns, lat_channels
    )
    latent = (
        (noisy.astype(jnp.float32) - step_size[0] * latent_field.astype(jnp.float32)) * latent_std
        + latent_mean
    ).astype(jnp.bfloat16)
    latent_wide = padded_2(latent, (("section", 2),), 2)
    earlier = passed_along(latent_wide, "sp", 1)
    stacked = pad_rows(jnp.concatenate([earlier, latent_wide], axis=0))
    extended = (conv_taps(stacked, in_weight, frames + 2, height, columns + 2) + in_bias).astype(
        jnp.bfloat16
    )
    extended = extended.reshape(frames + 2, height, columns + 2, half_channels)
    upblock_half = extended[2:, :, 1 : columns + 1]
    extended_full = lax.all_gather(extended, "tp", axis=3, tiled=True)
    normed = activate(extended_full, norm_gain)
    frame_index = lax.axis_index("sp") * frames - 2 + jnp.arange(frames + 2, dtype=jnp.int32)
    column_index = (
        lax.axis_index("section") * columns - 1 + jnp.arange(columns + 2, dtype=jnp.int32)
    )
    inside_cols = (column_index >= 0) & (column_index < columns * sections)
    inside = (frame_index >= 0)[:, None, None, None] & inside_cols[None, None, :, None]
    conv_input = pad_rows(jnp.where(inside, normed, jnp.zeros_like(normed)))
    full_weight = lax.all_gather(conv_weight, "section", axis=1, tiled=True)
    mixed = conv_taps(conv_input, full_weight, frames, height, columns)
    decoded = (
        upblock_half.astype(jnp.float32).reshape(-1, half_channels) + mixed + conv_bias
    ).astype(jnp.bfloat16)
    return decoded.reshape(frames, height, columns, half_channels)


def head_kernel(hidden, modulation, time_embed, weight, in_bias, out):
    tokens = hidden.shape[0]
    outs = weight.shape[1]
    x = hidden[...].astype(F32)
    embed = time_embed[...]
    scale = 1.0 + (modulation[1:2, :] + embed)
    shift = modulation[0:1, :] + embed
    scaled = x * scale
    high = scaled.astype(BF16)
    low = (scaled - high.astype(F32)).astype(BF16)
    row = lax.broadcasted_iota(jnp.int32, (16, x.shape[1]), 0)
    scale_high = scale.astype(BF16).astype(F32)
    shift_high = shift.astype(BF16).astype(F32)
    extra = jnp.where(row == 0, scale_high, 0.0)
    extra = jnp.where(row == 1, scale - scale_high, extra)
    extra = jnp.where(row == 2, shift_high, extra)
    extra = jnp.where(row == 3, shift - shift_high, extra).astype(BF16)
    stacked = jnp.concatenate([high, low, extra], axis=0)
    sums = jnp.dot(stacked, weight[...], preferred_element_type=F32)
    out[0:tokens, 0:outs] = sums[0:tokens] + sums[tokens : 2 * tokens]
    first = jnp.sum(x, axis=1, keepdims=True)
    second = jnp.sum(x * x, axis=1, keepdims=True)
    lane = lax.broadcasted_iota(jnp.int32, (tokens, outs), 1)
    out[0:tokens, outs : 2 * outs] = jnp.where(lane == 0, first, second)
    base = 2 * tokens
    out[tokens : tokens + 1, 0:outs] = sums[base : base + 1] + sums[base + 1 : base + 2]
    out[tokens : tokens + 1, outs : 2 * outs] = sums[base + 2 : base + 3] + sums[base + 3 : base + 4]
    biases = in_bias.shape[0]
    out[tokens + 1 : tokens + 1 + biases, :] = in_bias[...]
    rest = out.shape[0] - tokens - 1 - biases
    out[tokens + 1 + biases :, :] = jnp.zeros((rest, out.shape[1]), F32)


def message_kernel(mine, other, bias, place, noisy, out, *, features, cells, channels):
    tokens, outs = place.shape[0], bias.shape[1]
    total = mine[...] + other[...]
    average = total[0:tokens, outs : outs + 1] / features
    variance = total[0:tokens, outs + 1 : outs + 2] / features - average * average
    inverse = lax.rsqrt(variance + 1e-06)
    scale_sum = total[tokens : tokens + 1, 0:outs]
    shift_sum = total[tokens : tokens + 1, outs : 2 * outs]
    velocity = inverse * (total[0:tokens, 0:outs] - average * scale_sum) + (shift_sum + bias[...])
    velocity = velocity.astype(BF16)
    spread = lax.dot_general(
        velocity, place[...], (((0,), (0,)), ((), ())), preferred_element_type=F32
    )
    field = spread[0:channels, 0:cells]
    for part in range(1, outs // channels):
        field = field + spread[
            part * channels : (part + 1) * channels, part * cells : (part + 1) * cells
        ]
    out[:, 0:cells] = field.astype(BF16)
    out[:, cells:] = noisy[...]


def latent_kernel(where, step, *refs, sections, cells):
    messages, (std, mean, out, ordered) = refs[:sections], refs[sections:]
    mine = where[0]
    for k in range(sections):
        ordered[mine ^ k] = messages[k][...].astype(F32)
    tile = cells // sections
    for frame in range(sections):
        noisy = jnp.concatenate(
            [
                ordered[s, :, cells + frame * tile : cells + (frame + 1) * tile]
                for s in range(sections)
            ],
            axis=1,
        )
        field = ordered[frame, :, 0:cells]
        latent = (noisy - step[0] * field) * std[...] + mean[...]
        out[:, frame * cells : (frame + 1) * cells] = latent.astype(BF16)


def block_kernel(
    where, earlier, latent, weight_mine, weight_other, sums_mine, sums_other, gain, conv_hbm,
    *refs, frames, height, width, sections, tokens
):
    partials, (tile, rolled, blocks, normed, conv, arrived) = refs[:sections], refs[sections:]
    mine, block, first_frame = where[0], where[1], where[2]
    fetch = pltpu.make_async_copy(conv_hbm, conv, arrived)
    fetch.start()
    cells = height * width
    lat = latent.shape[0]
    lanes = 2 * frames * cells
    columns = width // sections
    half = weight_mine.shape[1]
    deep = gain.shape[2]
    per_half = half // deep
    x = jnp.concatenate([earlier[...].astype(F32), latent[...].astype(F32)], axis=1)
    position = lax.broadcasted_iota(jnp.int32, (1, lanes), 1)
    at_row = position % height
    at_column = (position // height) % width
    for b in range(3):
        for e in range(3):
            offset = (e - 1) * height + (b - 1)
            moved = x if offset == 0 else pltpu.roll(x, (-offset) % lanes, axis=1)
            row, column = at_row + (b - 1), at_column + (e - 1)
            inside = (row >= 0) & (row < height) & (column >= 0) & (column < width)
            moved = jnp.where(inside, moved, 0.0)
            first = (3 * b + e) * lat
            rolled[first : first + lat, :] = moved.astype(BF16)
    bias_rows = [
        source[tokens + 1 + i : tokens + 2 + i, :]
        for source in (sums_mine, sums_other)
        for i in range(per_half)
    ]
    gain_row = gain[mine]
    edge = lax.broadcasted_iota(jnp.int32, (cells, 1), 0) % height
    zero_column = jnp.zeros((height, deep), BF16)
    for frame in range(frames + 2):
        stacked = jnp.concatenate(
            [rolled[:, (frame + a) * cells : (frame + a + 1) * cells] for a in range(3)], axis=0
        )
        squares = jnp.zeros((cells, deep), F32)
        for which, weight in enumerate((weight_mine, weight_other)):
            product = lax.dot_general(
                stacked, weight[...], (((0,), (0,)), ((), ())), preferred_element_type=F32
            )
            for i in range(per_half):
                n = which * per_half + i
                piece = (product[:, i * deep : (i + 1) * deep] + bias_rows[n]).astype(BF16)
                blocks[n] = piece
                wide = piece.astype(F32)
                squares = squares + wide * wide
        mean = jnp.sum(squares, axis=1, keepdims=True) / (2 * half)
        inverse = lax.rsqrt(mean + 1e-06)
        value = blocks[block].astype(F32) * inverse * gain_row
        value = value / (1.0 + jnp.exp(-value))
        if frame < 2:
            value = jnp.where(first_frame + frame >= 0, value, 0.0)
        above = jnp.where(edge == 0, 0.0, pltpu.roll(value, 1, axis=0))
        below = jnp.where(edge == height - 1, 0.0, pltpu.roll(value, cells - 1, axis=0))
        for b, shifted in enumerate((above, value, below)):
            normed[b, frame, 1 : width + 1] = shifted.astype(BF16).reshape(width, height, deep)
            normed[b, frame, 0] = zero_column
            normed[b, frame, width + 1] = zero_column
        if frame >= 2:
            rows = pl.ds(pl.multiple_of(mine * (columns * height), columns * height), columns * height)
            for i in range(per_half):
                tile[frame - 2, :, i * deep : (i + 1) * deep] = blocks[i, rows, :]
    fetch.wait()
    size = frames * columns * height
    for k in range(sections):
        first_column = (mine ^ k) * columns
        total = jnp.zeros((size, half), F32)
        for a in range(3):
            for b in range(3):
                window = jnp.concatenate(
                    [
                        normed[b, a : a + frames, pl.ds(first_column + e, columns)].reshape(size, deep)
                        for e in range(3)
                    ],
                    axis=1,
                )
                taps = conv[9 * a + 3 * b : 9 * a + 3 * b + 3].reshape(3 * deep, half)
                total = total + jnp.dot(window, taps, preferred_element_type=F32)
        partials[k][...] = total.astype(partials[k].dtype)


def finish_kernel(tile, bias, order, *refs):
    parts, out = refs[:-1], refs[-1]
    rows = tile.shape[1]
    for frame in range(tile.shape[0]):
        total = tile[frame].astype(F32) + bias[...]
        for part in parts:
            total = total + part[frame * rows : (frame + 1) * rows, :].astype(F32)
        placed = jnp.dot(order[...], total.astype(BF16), preferred_element_type=F32)
        out[frame * rows : (frame + 1) * rows, :] = placed.astype(BF16)


def vmem(count):
    return [pl.BlockSpec(memory_space=pltpu.VMEM)] * count


SMEM = pl.BlockSpec(memory_space=pltpu.SMEM)


def call(kernel, shapes, in_specs, scratch=()):
    single = not isinstance(shapes, (list, tuple))
    specs = pl.BlockSpec(memory_space=pltpu.VMEM) if single else vmem(len(shapes))
    return pl.pallas_call(
        kernel, out_shape=shapes, in_specs=in_specs, out_specs=specs, scratch_shapes=list(scratch)
    )


def token_places(height, width):
    cells = height * width
    table = np.zeros((cells // 4, 4, cells), np.float32)
    for i in range(height // 2):
        for j in range(width // 2):
            for p in range(2):
                for q in range(2):
                    cell = (2 * j + q) * height + 2 * i + p
                    table[i * (width // 2) + j, 2 * p + q, cell] = 1.0
    return table.reshape(cells // 4, 4 * cells)


def row_order(height, columns):
    table = np.zeros((height * columns, height * columns), np.float32)
    for h in range(height):
        for w in range(columns):
            table[h * columns + w, w * height + h] = 1.0
    return table


def sectioned_shards(
    hidden, modulation, time_embed, head_weight, head_bias, noisy, step_size,
    latent_mean, latent_std, in_weight, in_bias, norm_gain, conv_weight, conv_bias,
):
    frames, height, columns, lat = noisy.shape
    sections, halves = lax.axis_size("section"), lax.axis_size("tp")
    width, half = columns * sections, in_weight.shape[2]
    cells = height * width
    tokens, local = hidden.shape
    outs = head_weight.shape[1]
    deep = conv_weight.shape[1]
    per_half = half // deep
    mine, side = lax.axis_index("section"), lax.axis_index("tp")
    swap = [(i, i ^ 1) for i in range(halves)]
    taps = in_weight.shape[0]

    weight_mine = in_weight.reshape(taps * lat, half)
    weight_other = lax.ppermute(weight_mine, "tp", swap)
    noisy_rows = jnp.transpose(noisy, (3, 0, 2, 1)).reshape(lat, frames * columns * height)
    sums = call(
        head_kernel, jax.ShapeDtypeStruct((tokens + 8, 2 * outs), F32), vmem(5)
    )(hidden, modulation, time_embed.reshape(1, local), head_weight, in_bias.reshape(per_half, deep))
    sums_other = lax.ppermute(sums, "tp", swap)

    place = jnp.asarray(token_places(height, width), BF16)
    message = call(
        lambda *refs: message_kernel(
            *refs, features=local * halves, cells=cells, channels=lat
        ),
        jax.ShapeDtypeStruct((lat, 2 * cells), BF16), vmem(5),
    )(sums, sums_other, head_bias.reshape(1, outs), place, noisy_rows)
    messages = [message] + [
        lax.ppermute(message, "section", [(i, i ^ k) for i in range(sections)])
        for k in range(1, sections)
    ]
    block = jnp.where((mine // per_half) == side, 0, per_half) + mine % per_half
    where = jnp.stack([mine, block, lax.axis_index("sp") * frames - 2]).astype(jnp.int32)
    latent = call(
        lambda *refs: latent_kernel(*refs, sections=sections, cells=cells),
        jax.ShapeDtypeStruct((lat, frames * cells), BF16),
        [SMEM, SMEM] + vmem(sections + 2),
        [pltpu.VMEM((sections, lat, 2 * cells), F32)],
    )(where, step_size, *messages, latent_std.reshape(lat, 1), latent_mean.reshape(lat, 1))
    earlier = passed_along(latent, "sp", 1)

    size = frames * columns * height
    results = call(
        lambda *refs: block_kernel(
            *refs, frames=frames, height=height, width=width, sections=sections, tokens=tokens
        ),
        [jax.ShapeDtypeStruct((size, half), F32 if k == 0 else BF16) for k in range(sections)]
        + [jax.ShapeDtypeStruct((frames, columns * height, half), BF16)],
        [SMEM] + vmem(7) + [pl.BlockSpec(memory_space=pl.ANY)],
        [
            pltpu.VMEM((9 * lat, 2 * frames * cells), BF16),
            pltpu.VMEM((sections, cells, deep), BF16),
            pltpu.VMEM((3, frames + 2, width + 2, height, deep), BF16),
            pltpu.VMEM(conv_weight.shape, BF16),
            pltpu.SemaphoreType.DMA(()),
        ],
    )(
        where, earlier, latent, weight_mine, weight_other, sums, sums_other,
        norm_gain.reshape(sections, 1, deep), conv_weight,
    )
    partials, tile = results[:sections], results[sections]
    received = {}
    for k in (2, 1, 3) if sections == 4 else range(1, sections):
        received[k] = lax.ppermute(partials[k], "section", [(i, i ^ k) for i in range(sections)])
    order = jnp.asarray(row_order(height, columns), BF16)
    decoded = call(
        finish_kernel, jax.ShapeDtypeStruct((size, half), BF16), vmem(3 + sections)
    )(
        tile, conv_bias.reshape(1, half), order, partials[0],
        *[received[k] for k in range(1, sections)],
    )
    return decoded.reshape(frames, height, columns, half)


def sectioned(mesh):
    def fits(hidden, noisy, in_weight, conv_weight):
        frames, height, columns, _ = noisy.shape
        sections = mesh.shape["section"]
        cells = height * columns * sections
        deep = conv_weight.shape[1]
        return (
            sections == frames
            and sections & (sections - 1) == 0
            and hidden.shape[0] * 4 == cells
            and mesh.shape["tp"] == 2
            and in_weight.shape[2] == 2 * deep
            and 2 * in_weight.shape[2] == sections * deep
            and deep % 128 == 0
            and height % 16 == 0
            and cells % 128 == 0
        )
    return fits


def solution(mesh):
    placed = (
        P(("groups", "sp", "section"), "tp"),
        P(None, "tp"),
        P(("groups", "tp")),
        P("tp", None),
        P(),
        P(("groups", "sp"), None, "section", None),
        P("groups"),
        P(),
        P(),
        P(None, None, "tp"),
        P("tp"),
        P(),
        P(None, "section", "tp"),
        P("tp"),
    )
    fits = sectioned(mesh)

    def shards(*args):
        body = sectioned_shards if fits(args[0], args[5], args[9], args[12]) else general_shards
        return body(*args)

    return jax.shard_map(
        shards,
        mesh=mesh,
        in_specs=placed,
        out_specs=P(("groups", "sp"), None, "section", "tp"),
        check_vma=False,
    )
```

```python
import jax
import jax.numpy as jnp
import numpy as np
from jax import lax
from jax.experimental import pallas as pl
from jax.experimental.pallas import tpu as pltpu
from jax.sharding import PartitionSpec as P

F32 = jnp.float32
BF16 = jnp.bfloat16


def padded_2(value, sides, width):
    for axis, dim in sides:
        count, length = (lax.axis_size(axis), value.shape[dim])
        up = [(i, (i + 1) % count) for i in range(count - 1)]
        down = [(j, i) for i, j in up]
        last = lax.slice_in_dim(value, length - width, length, axis=dim)
        leading = lax.slice_in_dim(value, 0, width, axis=dim)
        before = lax.ppermute(last, axis, up)
        after = lax.ppermute(leading, axis, down)
        value = jnp.concatenate([before, value, after], axis=dim)
    return value


def passed_along(value, axis, by):
    count = lax.axis_size(axis)
    pairs = [(i, i + by) for i in range(count) if 0 <= i + by < count]
    return lax.ppermute(value, axis, pairs)


def conv_taps(padded, weight, frames, height, columns):
    channels = padded.shape[3]
    result = jnp.zeros((frames * height * columns, weight.shape[2]), jnp.float32)
    for offset_time in range(3):
        for offset_row in range(3):
            slab = padded[offset_time : offset_time + frames, offset_row : offset_row + height]
            window = jnp.concatenate(
                [slab[:, :, 0:columns], slab[:, :, 1 : columns + 1], slab[:, :, 2 : columns + 2]],
                axis=3,
            )
            first = 9 * offset_time + 3 * offset_row
            taps = weight[first : first + 3].reshape(3 * channels, weight.shape[2])
            result = result + jnp.dot(
                window.reshape(-1, 3 * channels), taps, preferred_element_type=jnp.float32
            )
    return result


def activate(source, gain_vector):
    values = source.astype(jnp.float32)
    squares = jnp.mean(values * values, axis=-1, keepdims=True)
    return jax.nn.silu(values * lax.rsqrt(squares + 1e-06) * gain_vector).astype(jnp.bfloat16)


def pad_rows(source):
    return jnp.pad(source, ((0, 0), (1, 1), (0, 0), (0, 0)))


def general_shards(
    hidden, modulation, time_embed, head_weight, head_bias, noisy, step_size,
    latent_mean, latent_std, in_weight, in_bias, norm_gain, conv_weight, conv_bias,
):
    frames, height, columns, lat_channels = noisy.shape
    sections = lax.axis_size("section")
    half_channels = in_weight.shape[2]
    features = hidden.shape[1] * lax.axis_size("tp")
    values = hidden.astype(jnp.float32)
    row_sums, square_sums = lax.psum(
        (jnp.sum(values, axis=1), jnp.sum(values * values, axis=1)), "tp"
    )
    average = row_sums / features
    variance = square_sums / features - average * average
    shift_term = modulation[0] + time_embed
    scale_term = modulation[1] + time_embed
    modulated = (
        (values - average[:, None]) * lax.rsqrt(variance[:, None] + 1e-06) * (1.0 + scale_term)
        + shift_term
    ).astype(jnp.bfloat16)
    partial_sum = jnp.dot(modulated, head_weight, preferred_element_type=jnp.float32)
    velocity = (lax.psum(partial_sum, "tp") + head_bias).astype(jnp.bfloat16)
    band_rows = velocity.shape[0] * 2 // (columns * sections)
    outgoing = velocity.reshape(band_rows, sections, -1)
    arrived = lax.all_to_all(outgoing, "section", split_axis=1, concat_axis=0, tiled=True)
    latent_field = arrived.reshape(frames, height // 2, columns // 2, 2, 2, lat_channels)
    latent_field = jnp.transpose(latent_field, (0, 1, 3, 2, 4, 5)).reshape(
        frames, height, columns, lat_channels
    )
    latent = (
        (noisy.astype(jnp.float32) - step_size[0] * latent_field.astype(jnp.float32)) * latent_std
        + latent_mean
    ).astype(jnp.bfloat16)
    latent_wide = padded_2(latent, (("section", 2),), 2)
    earlier = passed_along(latent_wide, "sp", 1)
    stacked = pad_rows(jnp.concatenate([earlier, latent_wide], axis=0))
    extended = (conv_taps(stacked, in_weight, frames + 2, height, columns + 2) + in_bias).astype(
        jnp.bfloat16
    )
    extended = extended.reshape(frames + 2, height, columns + 2, half_channels)
    upblock_half = extended[2:, :, 1 : columns + 1]
    extended_full = lax.all_gather(extended, "tp", axis=3, tiled=True)
    normed = activate(extended_full, norm_gain)
    frame_index = lax.axis_index("sp") * frames - 2 + jnp.arange(frames + 2, dtype=jnp.int32)
    column_index = (
        lax.axis_index("section") * columns - 1 + jnp.arange(columns + 2, dtype=jnp.int32)
    )
    inside_cols = (column_index >= 0) & (column_index < columns * sections)
    inside = (frame_index >= 0)[:, None, None, None] & inside_cols[None, None, :, None]
    conv_input = pad_rows(jnp.where(inside, normed, jnp.zeros_like(normed)))
    full_weight = lax.all_gather(conv_weight, "section", axis=1, tiled=True)
    mixed = conv_taps(conv_input, full_weight, frames, height, columns)
    decoded = (
        upblock_half.astype(jnp.float32).reshape(-1, half_channels) + mixed + conv_bias
    ).astype(jnp.bfloat16)
    return decoded.reshape(frames, height, columns, half_channels)


def head_kernel(
    hidden_hbm, modulation_hbm, embed_hbm, weight_hbm, bias_hbm, out,
    hidden, modulation, time_embed, weight, in_bias, arrived, *, parts
):
    tokens, features = hidden.shape
    outs = weight.shape[0]
    wide = features // parts
    small = [
        pltpu.make_async_copy(source, target, arrived.at[i])
        for i, (source, target) in enumerate(
            ((modulation_hbm, modulation), (embed_hbm, time_embed), (bias_hbm, in_bias))
        )
    ]
    large = []
    for part in range(parts):
        cut = pl.ds(part * wide, wide)
        large.append(
            [
                pltpu.make_async_copy(
                    source.at[:, cut], target.at[:, cut], arrived.at[3 + 2 * part + i]
                )
                for i, (source, target) in enumerate(((hidden_hbm, hidden), (weight_hbm, weight)))
            ]
        )
    for copy in small + [copy for pair in large for copy in pair]:
        copy.start()
    for copy in small:
        copy.wait()
    sums, first, second = 0.0, 0.0, 0.0
    row = lax.broadcasted_iota(jnp.int32, (16, wide), 0)
    for part in range(parts):
        for copy in large[part]:
            copy.wait()
        cut = slice(part * wide, (part + 1) * wide)
        x = hidden[:, cut].astype(F32)
        embed = time_embed[:, cut]
        scale = 1.0 + (modulation[1:2, cut] + embed)
        shift = modulation[0:1, cut] + embed
        scaled = x * scale
        high = scaled.astype(BF16)
        low = (scaled - high.astype(F32)).astype(BF16)
        scale_high = scale.astype(BF16).astype(F32)
        shift_high = shift.astype(BF16).astype(F32)
        extra = jnp.where(row == 0, scale_high, 0.0)
        extra = jnp.where(row == 1, scale - scale_high, extra)
        extra = jnp.where(row == 2, shift_high, extra)
        extra = jnp.where(row == 3, shift - shift_high, extra).astype(BF16)
        stacked = jnp.concatenate([high, low, extra], axis=0)
        sums = sums + lax.dot_general(
            stacked, weight[:, cut], (((1,), (1,)), ((), ())), preferred_element_type=F32
        )
        first = first + jnp.sum(x, axis=1, keepdims=True)
        second = second + jnp.sum(x * x, axis=1, keepdims=True)
    out[0:tokens, 0:outs] = sums[0:tokens] + sums[tokens : 2 * tokens]
    lane = lax.broadcasted_iota(jnp.int32, (tokens, outs), 1)
    out[0:tokens, outs : 2 * outs] = jnp.where(lane == 0, first, second)
    base = 2 * tokens
    out[tokens : tokens + 1, 0:outs] = sums[base : base + 1] + sums[base + 1 : base + 2]
    out[tokens : tokens + 1, outs : 2 * outs] = sums[base + 2 : base + 3] + sums[base + 3 : base + 4]
    biases = in_bias.shape[0]
    out[tokens + 1 : tokens + 1 + biases, :] = in_bias[...]
    rest = out.shape[0] - tokens - 1 - biases
    out[tokens + 1 + biases :, :] = jnp.zeros((rest, out.shape[1]), F32)


def stage_kernel(_, *refs):
    count = (len(refs) - 1) // 2
    copies = [
        pltpu.make_async_copy(source, target, refs[-1].at[i])
        for i, (source, target) in enumerate(zip(refs[:count], refs[count:-1], strict=True))
    ]
    for copy in copies:
        copy.start()
    for copy in copies:
        copy.wait()


def message_kernel(mine, other, bias, place, noisy, out, *, features, cells, channels):
    tokens, outs = place.shape[0], bias.shape[1]
    total = mine[...] + other[...]
    average = total[0:tokens, outs : outs + 1] / features
    variance = total[0:tokens, outs + 1 : outs + 2] / features - average * average
    inverse = lax.rsqrt(variance + 1e-06)
    scale_sum = total[tokens : tokens + 1, 0:outs]
    shift_sum = total[tokens : tokens + 1, outs : 2 * outs]
    velocity = inverse * (total[0:tokens, 0:outs] - average * scale_sum) + (shift_sum + bias[...])
    velocity = velocity.astype(BF16)
    spread = lax.dot_general(
        velocity, place[...], (((0,), (0,)), ((), ())), preferred_element_type=F32
    )
    field = spread[0:channels, 0:cells]
    for part in range(1, outs // channels):
        field = field + spread[
            part * channels : (part + 1) * channels, part * cells : (part + 1) * cells
        ]
    for target in range(out.shape[0]):
        out[target, :, 0:cells] = field.astype(BF16)
        out[target, :, cells:] = noisy[...]


def latents(messages, first, step, std, mean, sections, members, cells):
    lat = std.shape[1]
    diagonal = lax.broadcasted_iota(jnp.int32, (lat, lat), 0) == lax.broadcasted_iota(
        jnp.int32, (lat, lat), 1
    )
    deviation = jnp.sum(jnp.where(diagonal, std[...], 0.0), axis=1, keepdims=True)
    middle = jnp.sum(jnp.where(diagonal, mean[...], 0.0), axis=1, keepdims=True)
    parts = [messages[first + s * members].astype(F32) for s in range(sections)]
    tile = cells // sections
    frames = []
    for frame in range(sections):
        cut = slice(cells + frame * tile, cells + (frame + 1) * tile)
        noisy = jnp.concatenate([part[:, cut] for part in parts], axis=1)
        latent = (noisy - step * parts[frame][:, 0:cells]) * deviation + middle
        frames.append(latent.astype(BF16).astype(F32))
    return jnp.concatenate(frames, axis=1)


def conv_tile(normed, conv, first_column, columns, frames):
    height, deep = normed.shape[3:]
    half = conv.shape[2]
    size = frames * columns * height
    total = jnp.zeros((size, half), F32)
    for a in range(3):
        for b in range(3):
            window = jnp.concatenate(
                [
                    normed[b, a : a + frames, pl.ds(first_column + e, columns)].reshape(size, deep)
                    for e in range(3)
                ],
                axis=1,
            )
            taps = conv[9 * a + 3 * b : 9 * a + 3 * b + 3].reshape(3 * deep, half)
            total = total + jnp.dot(window, taps, preferred_element_type=F32)
    return total


def norm_kernel(
    where, step, messages, std, mean, weight_mine, weight_other, sums_mine, sums_other, gain, conv,
    partial, tile, normed, rolled, blocks, *, frames, height, width, tokens, k, sections, members
):
    mine, block, member = where[0], where[1], where[2]
    first_frame = member * frames - 2
    cells = height * width
    lat = messages.shape[1]
    lanes = 2 * frames * cells
    half = weight_mine.shape[1]
    deep = gain.shape[2]
    columns = tile.shape[1] // height
    per_half = half // deep
    rest = (step[0], std, mean, sections, members, cells)
    earlier = latents(messages, jnp.maximum(member - 1, 0), *rest)
    earlier = jnp.where(member > 0, earlier, 0.0)
    x = jnp.concatenate([earlier, latents(messages, member, *rest)], axis=1)
    position = lax.broadcasted_iota(jnp.int32, (1, lanes), 1)
    at_row = position % height
    at_column = (position // height) % width
    for b in range(3):
        for e in range(3):
            offset = (e - 1) * height + (b - 1)
            moved = x if offset == 0 else pltpu.roll(x, (-offset) % lanes, axis=1)
            row, column = at_row + (b - 1), at_column + (e - 1)
            inside = (row >= 0) & (row < height) & (column >= 0) & (column < width)
            moved = jnp.where(inside, moved, 0.0)
            first = (3 * b + e) * lat
            rolled[first : first + lat, :] = moved.astype(BF16)
    bias_rows = [
        source[tokens + 1 + i : tokens + 2 + i, :]
        for source in (sums_mine, sums_other)
        for i in range(per_half)
    ]
    gain_row = gain[mine]
    edge = lax.broadcasted_iota(jnp.int32, (cells, 1), 0) % height
    zero_column = jnp.zeros((height, deep), BF16)
    for frame in range(frames + 2):
        stacked = jnp.concatenate(
            [rolled[:, (frame + a) * cells : (frame + a + 1) * cells] for a in range(3)], axis=0
        )
        squares = jnp.zeros((cells, deep), F32)
        for which, weight in enumerate((weight_mine, weight_other)):
            product = lax.dot_general(
                stacked, weight[...], (((0,), (0,)), ((), ())), preferred_element_type=F32
            )
            for i in range(per_half):
                n = which * per_half + i
                piece = (product[:, i * deep : (i + 1) * deep] + bias_rows[n]).astype(BF16)
                blocks[n] = piece
                wide = piece.astype(F32)
                squares = squares + wide * wide
        mean = jnp.sum(squares, axis=1, keepdims=True) / (2 * half)
        inverse = lax.rsqrt(mean + 1e-06)
        value = blocks[block].astype(F32) * inverse * gain_row
        value = value / (1.0 + jnp.exp(-value))
        if frame < 2:
            value = jnp.where(first_frame + frame >= 0, value, 0.0)
        above = jnp.where(edge == 0, 0.0, pltpu.roll(value, 1, axis=0))
        below = jnp.where(edge == height - 1, 0.0, pltpu.roll(value, cells - 1, axis=0))
        for b, shifted in enumerate((above, value, below)):
            normed[b, frame, 1 : width + 1] = shifted.astype(BF16).reshape(width, height, deep)
            normed[b, frame, 0] = zero_column
            normed[b, frame, width + 1] = zero_column
        if frame >= 2:
            rows = pl.ds(pl.multiple_of(mine * (columns * height), columns * height), columns * height)
            for i in range(per_half):
                tile[frame - 2, :, i * deep : (i + 1) * deep] = blocks[i, rows, :]
    partial[...] = conv_tile(normed, conv, (mine ^ k) * columns, columns, frames).astype(BF16)


def tile_kernel(where, normed, conv, partial, *, columns, frames, k):
    partial[...] = conv_tile(normed, conv, (where[0] ^ k) * columns, columns, frames).astype(
        partial.dtype
    )


def finish_kernel(tile, bias, order, *refs):
    parts, out = refs[:-1], refs[-1]
    rows, (height, columns) = tile.shape[1], out.shape[1:3]
    for frame in range(tile.shape[0]):
        total = tile[frame].astype(F32) + bias[...]
        for part in parts:
            total = total + part[frame * rows : (frame + 1) * rows, :].astype(F32)
        placed = jnp.dot(order[...], total.astype(BF16), preferred_element_type=F32)
        out[frame] = placed.reshape(height, columns, -1).astype(BF16)


def vmem(count):
    return [pl.BlockSpec(memory_space=pltpu.VMEM)] * count


SMEM = pl.BlockSpec(memory_space=pltpu.SMEM)
HBM = pl.BlockSpec(memory_space=pltpu.HBM)


VMEM_LIMIT = 12 * 2**20


def call(kernel, shapes, in_specs, scratch=(), last=False):
    single = not isinstance(shapes, (list, tuple))
    specs = pl.BlockSpec(memory_space=pltpu.VMEM) if single else vmem(len(shapes))
    if not last:
        local = [pltpu.VMEM(s.shape, s.dtype) for s in ([shapes] if single else shapes)]
        shapes = local[0] if single else local
    run = pl.pallas_call(
        kernel, out_shape=shapes, in_specs=in_specs, out_specs=specs, scratch_shapes=list(scratch),
        compiler_params=pltpu.CompilerParams(vmem_limit_bytes=VMEM_LIMIT),
    )

    def constrained(*args):
        return run(
            *[
                arg if spec is SMEM else pltpu.with_memory_space_constraint(arg, spec.memory_space)
                for arg, spec in zip(args, in_specs, strict=True)
            ]
        )

    return constrained


def staged(after, *arrays):
    return call(
        stage_kernel, [jax.ShapeDtypeStruct(x.shape, x.dtype) for x in arrays],
        vmem(1) + [HBM] * len(arrays), [pltpu.SemaphoreType.DMA((len(arrays),))],
    )(after, *arrays)


def token_places(height, width):
    cells = height * width
    table = np.zeros((cells // 4, 4, cells), np.float32)
    for i in range(height // 2):
        for j in range(width // 2):
            for p in range(2):
                for q in range(2):
                    cell = (2 * j + q) * height + 2 * i + p
                    table[i * (width // 2) + j, 2 * p + q, cell] = 1.0
    return table.reshape(cells // 4, 4 * cells)


def row_order(height, columns):
    table = np.zeros((height * columns, height * columns), np.float32)
    for h in range(height):
        for w in range(columns):
            table[h * columns + w, w * height + h] = 1.0
    return table


def sectioned_shards(
    hidden, modulation, time_embed, head_weight, head_bias, noisy, step_size,
    latent_mean, latent_std, in_weight, in_bias, norm_gain, conv_weight, conv_bias,
):
    frames, height, columns, lat = noisy.shape
    sections, halves = lax.axis_size("section"), lax.axis_size("tp")
    members = lax.axis_size("sp")
    width, half = columns * sections, in_weight.shape[2]
    cells = height * width
    tokens, local = hidden.shape
    outs = head_weight.shape[1]
    deep = conv_weight.shape[1]
    per_half = half // deep
    mine, side = lax.axis_index("section"), lax.axis_index("tp")
    swap = [(i, i ^ 1) for i in range(halves)]
    taps = in_weight.shape[0]

    noisy_rows = jnp.transpose(noisy, (3, 0, 2, 1)).reshape(lat, frames * columns * height)
    parts = 3 if local % (3 * 128) == 0 else 1
    head_in = (
        hidden, modulation, time_embed.reshape(1, local), head_weight.T,
        in_bias.reshape(per_half, deep),
    )
    sums = call(
        lambda *refs: head_kernel(*refs, parts=parts),
        jax.ShapeDtypeStruct((tokens + 8, 2 * outs), F32), [HBM] * 5,
        [pltpu.VMEM(x.shape, x.dtype) for x in head_in]
        + [pltpu.SemaphoreType.DMA((3 + 2 * parts,))],
    )(*head_in)
    sums_other = lax.ppermute(sums, "tp", swap)
    place, head_bias, latent_std, latent_mean, conv, weight_mine, gain, order, conv_bias = staged(
        sums, jnp.asarray(token_places(height, width), BF16), head_bias.reshape(1, outs),
        latent_std.reshape(1, lat), latent_mean.reshape(1, lat),
        conv_weight, in_weight.reshape(taps * lat, half),
        norm_gain.reshape(sections, 1, deep), jnp.asarray(row_order(height, columns), BF16),
        conv_bias.reshape(1, half),
    )
    weight_other = lax.ppermute(weight_mine, "tp", swap)
    message = call(
        lambda *refs: message_kernel(
            *refs, features=local * halves, cells=cells, channels=lat
        ),
        jax.ShapeDtypeStruct((sections * members, lat, 2 * cells), BF16), vmem(5),
    )(sums, sums_other, head_bias, place, noisy_rows)
    messages = lax.all_to_all(message, ("section", "sp"), 0, 0)
    block = jnp.where((mine // per_half) == side, 0, per_half) + mine % per_half
    where = jnp.stack([mine, block, lax.axis_index("sp")]).astype(jnp.int32)

    size = frames * columns * height
    sends = list(range(1, sections))
    sends = sends[sections // 2 - 1 :] + sends[: sections // 2 - 1]
    partials = {}
    partials[sends[0]], tile, normed = call(
        lambda *refs: norm_kernel(
            *refs, frames=frames, height=height, width=width, tokens=tokens, k=sends[0],
            sections=sections, members=members
        ),
        [
            jax.ShapeDtypeStruct((size, half), BF16),
            jax.ShapeDtypeStruct((frames, columns * height, half), BF16),
            jax.ShapeDtypeStruct((3, frames + 2, width + 2, height, deep), BF16),
        ],
        [SMEM, SMEM] + vmem(9),
        [
            pltpu.VMEM((9 * lat, 2 * frames * cells), BF16),
            pltpu.VMEM((sections, cells, deep), BF16),
        ],
    )(
        where, step_size, messages, latent_std, latent_mean, weight_mine, weight_other, sums,
        sums_other, gain, conv,
    )
    received = {}
    for k in sends + [0]:
        if k not in partials:
            partials[k] = call(
                lambda *refs: tile_kernel(*refs, columns=columns, frames=frames, k=k),
                jax.ShapeDtypeStruct((size, half), BF16 if k else F32), [SMEM] + vmem(2),
            )(where, normed, conv)
        if k:
            received[k] = lax.ppermute(
                partials[k], "section", [(i, i ^ k) for i in range(sections)]
            )
    return call(
        finish_kernel, jax.ShapeDtypeStruct((frames, height, columns, half), BF16),
        vmem(3 + sections), last=True,
    )(tile, conv_bias, order, partials[0], *[received[k] for k in sends])


def sectioned(mesh):
    def fits(hidden, head_weight, noisy, in_weight, conv_weight):
        frames, height, columns, _ = noisy.shape
        sections = mesh.shape["section"]
        cells = height * columns * sections
        deep = conv_weight.shape[1]
        return (
            sections == frames
            and sections & (sections - 1) == 0
            and hidden.shape[0] * 4 == cells
            and mesh.shape["tp"] == 2
            and in_weight.shape[2] == 2 * deep
            and 2 * in_weight.shape[2] == sections * deep
            and deep % 128 == 0
            and 2 * head_weight.shape[1] == deep
            and height % 16 == 0
            and cells % 128 == 0
        )
    return fits


def solution(mesh):
    placed = (
        P(("groups", "sp", "section"), "tp"),
        P(None, "tp"),
        P(("groups", "tp")),
        P("tp", None),
        P(),
        P(("groups", "sp"), None, "section", None),
        P("groups"),
        P(),
        P(),
        P(None, None, "tp"),
        P("tp"),
        P(),
        P(None, "section", "tp"),
        P("tp"),
    )
    fits = sectioned(mesh)

    def shards(*args):
        body = sectioned_shards if fits(args[0], args[3], args[5], args[9], args[12]) else general_shards
        return body(*args)

    return jax.shard_map(
        shards,
        mesh=mesh,
        in_specs=placed,
        out_specs=P(("groups", "sp"), None, "section", "tp"),
        check_vma=False,
    )
```

```python
import jax
import jax.numpy as jnp
import numpy as np
from jax import lax
from jax.experimental import pallas as pl
from jax.experimental.pallas import tpu as pltpu
from jax.sharding import PartitionSpec as P

F32 = jnp.float32
BF16 = jnp.bfloat16


def padded_2(value, sides, width):
    for axis, dim in sides:
        count, length = (lax.axis_size(axis), value.shape[dim])
        up = [(i, (i + 1) % count) for i in range(count - 1)]
        down = [(j, i) for i, j in up]
        last = lax.slice_in_dim(value, length - width, length, axis=dim)
        leading = lax.slice_in_dim(value, 0, width, axis=dim)
        before = lax.ppermute(last, axis, up)
        after = lax.ppermute(leading, axis, down)
        value = jnp.concatenate([before, value, after], axis=dim)
    return value


def passed_along(value, axis, by):
    count = lax.axis_size(axis)
    pairs = [(i, i + by) for i in range(count) if 0 <= i + by < count]
    return lax.ppermute(value, axis, pairs)


def conv_taps(padded, weight, frames, height, columns):
    channels = padded.shape[3]
    result = jnp.zeros((frames * height * columns, weight.shape[2]), jnp.float32)
    for offset_time in range(3):
        for offset_row in range(3):
            slab = padded[offset_time : offset_time + frames, offset_row : offset_row + height]
            window = jnp.concatenate(
                [slab[:, :, 0:columns], slab[:, :, 1 : columns + 1], slab[:, :, 2 : columns + 2]],
                axis=3,
            )
            first = 9 * offset_time + 3 * offset_row
            taps = weight[first : first + 3].reshape(3 * channels, weight.shape[2])
            result = result + jnp.dot(
                window.reshape(-1, 3 * channels), taps, preferred_element_type=jnp.float32
            )
    return result


def activate(source, gain_vector):
    values = source.astype(jnp.float32)
    squares = jnp.mean(values * values, axis=-1, keepdims=True)
    return jax.nn.silu(values * lax.rsqrt(squares + 1e-06) * gain_vector).astype(jnp.bfloat16)


def pad_rows(source):
    return jnp.pad(source, ((0, 0), (1, 1), (0, 0), (0, 0)))


def general_shards(
    hidden, modulation, time_embed, head_weight, head_bias, noisy, step_size,
    latent_mean, latent_std, in_weight, in_bias, norm_gain, conv_weight, conv_bias,
):
    frames, height, columns, lat_channels = noisy.shape
    sections = lax.axis_size("section")
    half_channels = in_weight.shape[2]
    features = hidden.shape[1] * lax.axis_size("tp")
    values = hidden.astype(jnp.float32)
    row_sums, square_sums = lax.psum(
        (jnp.sum(values, axis=1), jnp.sum(values * values, axis=1)), "tp"
    )
    average = row_sums / features
    variance = square_sums / features - average * average
    shift_term = modulation[0] + time_embed
    scale_term = modulation[1] + time_embed
    modulated = (
        (values - average[:, None]) * lax.rsqrt(variance[:, None] + 1e-06) * (1.0 + scale_term)
        + shift_term
    ).astype(jnp.bfloat16)
    partial_sum = jnp.dot(modulated, head_weight, preferred_element_type=jnp.float32)
    velocity = (lax.psum(partial_sum, "tp") + head_bias).astype(jnp.bfloat16)
    band_rows = velocity.shape[0] * 2 // (columns * sections)
    outgoing = velocity.reshape(band_rows, sections, -1)
    arrived = lax.all_to_all(outgoing, "section", split_axis=1, concat_axis=0, tiled=True)
    latent_field = arrived.reshape(frames, height // 2, columns // 2, 2, 2, lat_channels)
    latent_field = jnp.transpose(latent_field, (0, 1, 3, 2, 4, 5)).reshape(
        frames, height, columns, lat_channels
    )
    latent = (
        (noisy.astype(jnp.float32) - step_size[0] * latent_field.astype(jnp.float32)) * latent_std
        + latent_mean
    ).astype(jnp.bfloat16)
    latent_wide = padded_2(latent, (("section", 2),), 2)
    earlier = passed_along(latent_wide, "sp", 1)
    stacked = pad_rows(jnp.concatenate([earlier, latent_wide], axis=0))
    extended = (conv_taps(stacked, in_weight, frames + 2, height, columns + 2) + in_bias).astype(
        jnp.bfloat16
    )
    extended = extended.reshape(frames + 2, height, columns + 2, half_channels)
    upblock_half = extended[2:, :, 1 : columns + 1]
    extended_full = lax.all_gather(extended, "tp", axis=3, tiled=True)
    normed = activate(extended_full, norm_gain)
    frame_index = lax.axis_index("sp") * frames - 2 + jnp.arange(frames + 2, dtype=jnp.int32)
    column_index = (
        lax.axis_index("section") * columns - 1 + jnp.arange(columns + 2, dtype=jnp.int32)
    )
    inside_cols = (column_index >= 0) & (column_index < columns * sections)
    inside = (frame_index >= 0)[:, None, None, None] & inside_cols[None, None, :, None]
    conv_input = pad_rows(jnp.where(inside, normed, jnp.zeros_like(normed)))
    full_weight = lax.all_gather(conv_weight, "section", axis=1, tiled=True)
    mixed = conv_taps(conv_input, full_weight, frames, height, columns)
    decoded = (
        upblock_half.astype(jnp.float32).reshape(-1, half_channels) + mixed + conv_bias
    ).astype(jnp.bfloat16)
    return decoded.reshape(frames, height, columns, half_channels)


def head_kernel(
    hidden_hbm, modulation_hbm, embed_hbm, weight_hbm, bias_hbm, out,
    hidden, modulation, time_embed, weight, in_bias, arrived, *, parts
):
    tokens, features = hidden.shape
    outs = weight.shape[0]
    wide = features // parts
    small = [
        pltpu.make_async_copy(source, target, arrived.at[i])
        for i, (source, target) in enumerate(
            ((modulation_hbm, modulation), (embed_hbm, time_embed), (bias_hbm, in_bias))
        )
    ]
    large = []
    for part in range(parts):
        cut = pl.ds(part * wide, wide)
        large.append(
            [
                pltpu.make_async_copy(
                    source.at[:, cut], target.at[:, cut], arrived.at[3 + 2 * part + i]
                )
                for i, (source, target) in enumerate(((hidden_hbm, hidden), (weight_hbm, weight)))
            ]
        )
    for copy in small + [copy for pair in large for copy in pair]:
        copy.start()
    for copy in small:
        copy.wait()
    sums, first, second = 0.0, 0.0, 0.0
    row = lax.broadcasted_iota(jnp.int32, (16, wide), 0)
    for part in range(parts):
        for copy in large[part]:
            copy.wait()
        cut = slice(part * wide, (part + 1) * wide)
        x = hidden[:, cut].astype(F32)
        embed = time_embed[:, cut]
        scale = 1.0 + (modulation[1:2, cut] + embed)
        shift = modulation[0:1, cut] + embed
        scaled = x * scale
        high = scaled.astype(BF16)
        low = (scaled - high.astype(F32)).astype(BF16)
        scale_high = scale.astype(BF16).astype(F32)
        shift_high = shift.astype(BF16).astype(F32)
        extra = jnp.where(row == 0, scale_high, 0.0)
        extra = jnp.where(row == 1, scale - scale_high, extra)
        extra = jnp.where(row == 2, shift_high, extra)
        extra = jnp.where(row == 3, shift - shift_high, extra).astype(BF16)
        stacked = jnp.concatenate([high, low, extra], axis=0)
        sums = sums + lax.dot_general(
            stacked, weight[:, cut], (((1,), (1,)), ((), ())), preferred_element_type=F32
        )
        first = first + jnp.sum(x, axis=1, keepdims=True)
        second = second + jnp.sum(x * x, axis=1, keepdims=True)
    out[0:tokens, 0:outs] = sums[0:tokens] + sums[tokens : 2 * tokens]
    lane = lax.broadcasted_iota(jnp.int32, (tokens, outs), 1)
    out[0:tokens, outs : 2 * outs] = jnp.where(lane == 0, first, second)
    base = 2 * tokens
    out[tokens : tokens + 1, 0:outs] = sums[base : base + 1] + sums[base + 1 : base + 2]
    out[tokens : tokens + 1, outs : 2 * outs] = sums[base + 2 : base + 3] + sums[base + 3 : base + 4]
    biases = in_bias.shape[0]
    out[tokens + 1 : tokens + 1 + biases, :] = in_bias[...]
    rest = out.shape[0] - tokens - 1 - biases
    out[tokens + 1 + biases :, :] = jnp.zeros((rest, out.shape[1]), F32)


def stage_kernel(_, *refs):
    count = (len(refs) - 1) // 2
    copies = [
        pltpu.make_async_copy(source, target, refs[-1].at[i])
        for i, (source, target) in enumerate(zip(refs[:count], refs[count:-1], strict=True))
    ]
    for copy in copies:
        copy.start()
    for copy in copies:
        copy.wait()


def message_kernel(mine, other, bias, place, noisy, out, *, features, cells, channels):
    tokens, outs = place.shape[0], bias.shape[1]
    total = mine[...] + other[...]
    average = total[0:tokens, outs : outs + 1] / features
    variance = total[0:tokens, outs + 1 : outs + 2] / features - average * average
    inverse = lax.rsqrt(variance + 1e-06)
    scale_sum = total[tokens : tokens + 1, 0:outs]
    shift_sum = total[tokens : tokens + 1, outs : 2 * outs]
    velocity = inverse * (total[0:tokens, 0:outs] - average * scale_sum) + (shift_sum + bias[...])
    velocity = velocity.astype(BF16)
    spread = lax.dot_general(
        velocity, place[...], (((0,), (0,)), ((), ())), preferred_element_type=F32
    )
    field = spread[0:channels, 0:cells]
    for part in range(1, outs // channels):
        field = field + spread[
            part * channels : (part + 1) * channels, part * cells : (part + 1) * cells
        ]
    for target in range(out.shape[0]):
        out[target, :, 0:cells] = field.astype(BF16)
        out[target, :, cells:] = noisy[...]


def latents(messages, first, step, std, mean, sections, members, cells):
    lat = std.shape[1]
    diagonal = lax.broadcasted_iota(jnp.int32, (lat, lat), 0) == lax.broadcasted_iota(
        jnp.int32, (lat, lat), 1
    )
    deviation = jnp.sum(jnp.where(diagonal, std[...], 0.0), axis=1, keepdims=True)
    middle = jnp.sum(jnp.where(diagonal, mean[...], 0.0), axis=1, keepdims=True)
    parts = [messages[first + s * members].astype(F32) for s in range(sections)]
    tile = cells // sections
    frames = []
    for frame in range(sections):
        cut = slice(cells + frame * tile, cells + (frame + 1) * tile)
        noisy = jnp.concatenate([part[:, cut] for part in parts], axis=1)
        latent = (noisy - step * parts[frame][:, 0:cells]) * deviation + middle
        frames.append(latent.astype(BF16).astype(F32))
    return jnp.concatenate(frames, axis=1)


def conv_tile(normed, conv, first_column, columns, frames):
    height, deep = normed.shape[3:]
    half = conv.shape[2]
    size = frames * columns * height
    total = jnp.zeros((size, half), F32)
    for a in range(3):
        for b in range(3):
            window = jnp.concatenate(
                [
                    normed[b, a : a + frames, pl.ds(first_column + e, columns)].reshape(size, deep)
                    for e in range(3)
                ],
                axis=1,
            )
            taps = conv[9 * a + 3 * b : 9 * a + 3 * b + 3].reshape(3 * deep, half)
            total = total + jnp.dot(window, taps, preferred_element_type=F32)
    return total


def norm_kernel(
    where, step, messages, std, mean, weight_mine, weight_other, sums_mine, sums_other, gain, conv,
    partial, tile, normed, rolled, blocks, *, frames, height, width, tokens, k, sections, members
):
    mine, block, member = where[0], where[1], where[2]
    first_frame = member * frames - 2
    cells = height * width
    lat = messages.shape[1]
    lanes = 2 * frames * cells
    half = weight_mine.shape[1]
    deep = gain.shape[2]
    columns = tile.shape[1] // height
    per_half = half // deep
    rest = (step[0], std, mean, sections, members, cells)
    earlier = latents(messages, jnp.maximum(member - 1, 0), *rest)
    earlier = jnp.where(member > 0, earlier, 0.0)
    x = jnp.concatenate([earlier, latents(messages, member, *rest)], axis=1)
    position = lax.broadcasted_iota(jnp.int32, (1, lanes), 1)
    at_row = position % height
    at_column = (position // height) % width
    for b in range(3):
        for e in range(3):
            offset = (e - 1) * height + (b - 1)
            moved = x if offset == 0 else pltpu.roll(x, (-offset) % lanes, axis=1)
            row, column = at_row + (b - 1), at_column + (e - 1)
            inside = (row >= 0) & (row < height) & (column >= 0) & (column < width)
            moved = jnp.where(inside, moved, 0.0)
            first = (3 * b + e) * lat
            rolled[first : first + lat, :] = moved.astype(BF16)
    bias_rows = [
        source[tokens + 1 + i : tokens + 2 + i, :]
        for source in (sums_mine, sums_other)
        for i in range(per_half)
    ]
    gain_row = gain[mine]
    edge = lax.broadcasted_iota(jnp.int32, (cells, 1), 0) % height
    zero_column = jnp.zeros((height, deep), BF16)
    for frame in range(frames + 2):
        stacked = jnp.concatenate(
            [rolled[:, (frame + a) * cells : (frame + a + 1) * cells] for a in range(3)], axis=0
        )
        squares = jnp.zeros((cells, deep), F32)
        for which, weight in enumerate((weight_mine, weight_other)):
            product = lax.dot_general(
                stacked, weight[...], (((0,), (0,)), ((), ())), preferred_element_type=F32
            )
            for i in range(per_half):
                n = which * per_half + i
                piece = (product[:, i * deep : (i + 1) * deep] + bias_rows[n]).astype(BF16)
                blocks[n] = piece
                wide = piece.astype(F32)
                squares = squares + wide * wide
        mean = jnp.sum(squares, axis=1, keepdims=True) / (2 * half)
        inverse = lax.rsqrt(mean + 1e-06)
        value = blocks[block].astype(F32) * inverse * gain_row
        value = value / (1.0 + jnp.exp(-value))
        if frame < 2:
            value = jnp.where(first_frame + frame >= 0, value, 0.0)
        above = jnp.where(edge == 0, 0.0, pltpu.roll(value, 1, axis=0))
        below = jnp.where(edge == height - 1, 0.0, pltpu.roll(value, cells - 1, axis=0))
        for b, shifted in enumerate((above, value, below)):
            normed[b, frame, 1 : width + 1] = shifted.astype(BF16).reshape(width, height, deep)
            normed[b, frame, 0] = zero_column
            normed[b, frame, width + 1] = zero_column
        if frame >= 2:
            rows = pl.ds(pl.multiple_of(mine * (columns * height), columns * height), columns * height)
            for i in range(per_half):
                tile[frame - 2, :, i * deep : (i + 1) * deep] = blocks[i, rows, :]
    partial[...] = conv_tile(normed, conv, (mine ^ k) * columns, columns, frames).astype(BF16)


def tile_kernel(where, normed, conv, partial, *, columns, frames, k):
    partial[...] = conv_tile(normed, conv, (where[0] ^ k) * columns, columns, frames).astype(
        partial.dtype
    )


def finish_kernel(tile, bias, order, *refs):
    parts, out = refs[:-1], refs[-1]
    rows, (height, columns) = tile.shape[1], out.shape[1:3]
    for frame in range(tile.shape[0]):
        total = tile[frame].astype(F32) + bias[...]
        for part in parts:
            total = total + part[frame * rows : (frame + 1) * rows, :].astype(F32)
        placed = jnp.dot(order[...], total.astype(BF16), preferred_element_type=F32)
        out[frame] = placed.reshape(height, columns, -1).astype(BF16)


def vmem(count):
    return [pl.BlockSpec(memory_space=pltpu.VMEM)] * count


SMEM = pl.BlockSpec(memory_space=pltpu.SMEM)
HBM = pl.BlockSpec(memory_space=pltpu.HBM)


VMEM_LIMIT = 12 * 2**20


def call(kernel, shapes, in_specs, scratch=(), last=False):
    single = not isinstance(shapes, (list, tuple))
    specs = pl.BlockSpec(memory_space=pltpu.VMEM) if single else vmem(len(shapes))
    if not last:
        local = [pltpu.VMEM(s.shape, s.dtype) for s in ([shapes] if single else shapes)]
        shapes = local[0] if single else local
    run = pl.pallas_call(
        kernel, out_shape=shapes, in_specs=in_specs, out_specs=specs, scratch_shapes=list(scratch),
        compiler_params=pltpu.CompilerParams(vmem_limit_bytes=VMEM_LIMIT),
    )

    def constrained(*args):
        return run(
            *[
                arg if spec is SMEM else pltpu.with_memory_space_constraint(arg, spec.memory_space)
                for arg, spec in zip(args, in_specs, strict=True)
            ]
        )

    return constrained


def staged(after, *arrays):
    return call(
        stage_kernel, [jax.ShapeDtypeStruct(x.shape, x.dtype) for x in arrays],
        vmem(1) + [HBM] * len(arrays), [pltpu.SemaphoreType.DMA((len(arrays),))],
    )(after, *arrays)


def token_places(height, width):
    cells = height * width
    table = np.zeros((cells // 4, 4, cells), np.float32)
    for i in range(height // 2):
        for j in range(width // 2):
            for p in range(2):
                for q in range(2):
                    cell = (2 * j + q) * height + 2 * i + p
                    table[i * (width // 2) + j, 2 * p + q, cell] = 1.0
    return table.reshape(cells // 4, 4 * cells)


def row_order(height, columns):
    table = np.zeros((height * columns, height * columns), np.float32)
    for h in range(height):
        for w in range(columns):
            table[h * columns + w, w * height + h] = 1.0
    return table


def send_order(sections):
    return list(range(sections // 2, sections)) + list(range(1, sections // 2))


def sectioned_shards(
    hidden, modulation, time_embed, head_weight, head_bias, noisy, step_size,
    latent_mean, latent_std, in_weight, in_bias, norm_gain, conv_weight, conv_bias,
):
    frames, height, columns, lat = noisy.shape
    sections, halves = lax.axis_size("section"), lax.axis_size("tp")
    members = lax.axis_size("sp")
    width, half = columns * sections, in_weight.shape[2]
    cells = height * width
    tokens, local = hidden.shape
    outs = head_weight.shape[1]
    deep = conv_weight.shape[1]
    per_half = half // deep
    mine, side = lax.axis_index("section"), lax.axis_index("tp")
    swap = [(i, i ^ 1) for i in range(halves)]
    taps = in_weight.shape[0]

    noisy_rows = jnp.transpose(noisy, (3, 0, 2, 1)).reshape(lat, frames * columns * height)
    parts = 3 if local % (3 * 128) == 0 else 1
    head_in = (
        hidden, modulation, time_embed.reshape(1, local), head_weight.T,
        in_bias.reshape(per_half, deep),
    )
    sums = call(
        lambda *refs: head_kernel(*refs, parts=parts),
        jax.ShapeDtypeStruct((tokens + 8, 2 * outs), F32), [HBM] * 5,
        [pltpu.VMEM(x.shape, x.dtype) for x in head_in]
        + [pltpu.SemaphoreType.DMA((3 + 2 * parts,))],
    )(*head_in)
    sums_other = lax.ppermute(sums, "tp", swap)
    place, head_bias = staged(
        sums, jnp.asarray(token_places(height, width), BF16), head_bias.reshape(1, outs)
    )
    message = call(
        lambda *refs: message_kernel(
            *refs, features=local * halves, cells=cells, channels=lat
        ),
        jax.ShapeDtypeStruct((sections * members, lat, 2 * cells), BF16), vmem(5),
    )(sums, sums_other, head_bias, place, noisy_rows)
    messages = lax.all_to_all(message, ("section", "sp"), 0, 0)
    latent_std, latent_mean, conv, weight_mine, gain, order, conv_bias = staged(
        message, latent_std.reshape(1, lat), latent_mean.reshape(1, lat),
        conv_weight, in_weight.reshape(taps * lat, half),
        norm_gain.reshape(sections, 1, deep), jnp.asarray(row_order(height, columns), BF16),
        conv_bias.reshape(1, half),
    )
    weight_other = lax.ppermute(weight_mine, "tp", swap)
    block = jnp.where((mine // per_half) == side, 0, per_half) + mine % per_half
    where = jnp.stack([mine, block, lax.axis_index("sp")]).astype(jnp.int32)

    size = frames * columns * height
    sends = send_order(sections)
    partials = {}
    partials[sends[0]], tile, normed = call(
        lambda *refs: norm_kernel(
            *refs, frames=frames, height=height, width=width, tokens=tokens, k=sends[0],
            sections=sections, members=members
        ),
        [
            jax.ShapeDtypeStruct((size, half), BF16),
            jax.ShapeDtypeStruct((frames, columns * height, half), BF16),
            jax.ShapeDtypeStruct((3, frames + 2, width + 2, height, deep), BF16),
        ],
        [SMEM, SMEM] + vmem(9),
        [
            pltpu.VMEM((9 * lat, 2 * frames * cells), BF16),
            pltpu.VMEM((sections, cells, deep), BF16),
        ],
    )(
        where, step_size, messages, latent_std, latent_mean, weight_mine, weight_other, sums,
        sums_other, gain, conv,
    )
    received = {}
    for k in sends + [0]:
        if k not in partials:
            partials[k] = call(
                lambda *refs: tile_kernel(*refs, columns=columns, frames=frames, k=k),
                jax.ShapeDtypeStruct((size, half), BF16 if k else F32), [SMEM] + vmem(2),
            )(where, normed, conv)
        if k:
            received[k] = lax.ppermute(
                partials[k], "section", [(i, i ^ k) for i in range(sections)]
            )
    return call(
        finish_kernel, jax.ShapeDtypeStruct((frames, height, columns, half), BF16),
        vmem(3 + sections), last=True,
    )(tile, conv_bias, order, partials[0], *[received[k] for k in sends])


def sectioned(mesh):
    def fits(hidden, head_weight, noisy, in_weight, conv_weight):
        frames, height, columns, _ = noisy.shape
        sections = mesh.shape["section"]
        cells = height * columns * sections
        deep = conv_weight.shape[1]
        return (
            sections == frames
            and sections & (sections - 1) == 0
            and hidden.shape[0] * 4 == cells
            and mesh.shape["tp"] == 2
            and in_weight.shape[2] == 2 * deep
            and 2 * in_weight.shape[2] == sections * deep
            and deep % 128 == 0
            and 2 * head_weight.shape[1] == deep
            and height % 16 == 0
            and cells % 128 == 0
        )

    return fits


def solution(mesh):
    placed = (
        P(("groups", "sp", "section"), "tp"),
        P(None, "tp"),
        P(("groups", "tp")),
        P("tp", None),
        P(),
        P(("groups", "sp"), None, "section", None),
        P("groups"),
        P(),
        P(),
        P(None, None, "tp"),
        P("tp"),
        P(),
        P(None, "section", "tp"),
        P("tp"),
    )
    fits = sectioned(mesh)

    def shards(*args):
        if not fits(args[0], args[3], args[5], args[9], args[12]):
            return general_shards(*args)
        return sectioned_shards(*args)

    return jax.shard_map(
        shards,
        mesh=mesh,
        in_specs=placed,
        out_specs=P(("groups", "sp"), None, "section", "tp"),
        check_vma=False,
    )
```

```python
import jax
import jax.numpy as jnp
import numpy as np
from jax import lax
from jax.experimental import pallas as pl
from jax.experimental.pallas import tpu as pltpu
from jax.sharding import PartitionSpec as P

F32 = jnp.float32
BF16 = jnp.bfloat16


def padded_2(value, sides, width):
    for axis, dim in sides:
        count, length = (lax.axis_size(axis), value.shape[dim])
        up = [(i, (i + 1) % count) for i in range(count - 1)]
        down = [(j, i) for i, j in up]
        last = lax.slice_in_dim(value, length - width, length, axis=dim)
        leading = lax.slice_in_dim(value, 0, width, axis=dim)
        before = lax.ppermute(last, axis, up)
        after = lax.ppermute(leading, axis, down)
        value = jnp.concatenate([before, value, after], axis=dim)
    return value


def passed_along(value, axis, by):
    count = lax.axis_size(axis)
    pairs = [(i, i + by) for i in range(count) if 0 <= i + by < count]
    return lax.ppermute(value, axis, pairs)


def conv_taps(padded, weight, frames, height, columns):
    channels = padded.shape[3]
    result = jnp.zeros((frames * height * columns, weight.shape[2]), jnp.float32)
    for offset_time in range(3):
        for offset_row in range(3):
            slab = padded[offset_time : offset_time + frames, offset_row : offset_row + height]
            window = jnp.concatenate(
                [slab[:, :, 0:columns], slab[:, :, 1 : columns + 1], slab[:, :, 2 : columns + 2]],
                axis=3,
            )
            first = 9 * offset_time + 3 * offset_row
            taps = weight[first : first + 3].reshape(3 * channels, weight.shape[2])
            result = result + jnp.dot(
                window.reshape(-1, 3 * channels), taps, preferred_element_type=jnp.float32
            )
    return result


def activate(source, gain_vector):
    values = source.astype(jnp.float32)
    squares = jnp.mean(values * values, axis=-1, keepdims=True)
    return jax.nn.silu(values * lax.rsqrt(squares + 1e-06) * gain_vector).astype(jnp.bfloat16)


def pad_rows(source):
    return jnp.pad(source, ((0, 0), (1, 1), (0, 0), (0, 0)))


def general_shards(
    hidden, modulation, time_embed, head_weight, head_bias, noisy, step_size,
    latent_mean, latent_std, in_weight, in_bias, norm_gain, conv_weight, conv_bias,
):
    frames, height, columns, lat_channels = noisy.shape
    sections = lax.axis_size("section")
    half_channels = in_weight.shape[2]
    features = hidden.shape[1] * lax.axis_size("tp")
    values = hidden.astype(jnp.float32)
    row_sums, square_sums = lax.psum(
        (jnp.sum(values, axis=1), jnp.sum(values * values, axis=1)), "tp"
    )
    average = row_sums / features
    variance = square_sums / features - average * average
    shift_term = modulation[0] + time_embed
    scale_term = modulation[1] + time_embed
    modulated = (
        (values - average[:, None]) * lax.rsqrt(variance[:, None] + 1e-06) * (1.0 + scale_term)
        + shift_term
    ).astype(jnp.bfloat16)
    partial_sum = jnp.dot(modulated, head_weight, preferred_element_type=jnp.float32)
    velocity = (lax.psum(partial_sum, "tp") + head_bias).astype(jnp.bfloat16)
    band_rows = velocity.shape[0] * 2 // (columns * sections)
    outgoing = velocity.reshape(band_rows, sections, -1)
    arrived = lax.all_to_all(outgoing, "section", split_axis=1, concat_axis=0, tiled=True)
    latent_field = arrived.reshape(frames, height // 2, columns // 2, 2, 2, lat_channels)
    latent_field = jnp.transpose(latent_field, (0, 1, 3, 2, 4, 5)).reshape(
        frames, height, columns, lat_channels
    )
    latent = (
        (noisy.astype(jnp.float32) - step_size[0] * latent_field.astype(jnp.float32)) * latent_std
        + latent_mean
    ).astype(jnp.bfloat16)
    latent_wide = padded_2(latent, (("section", 2),), 2)
    earlier = passed_along(latent_wide, "sp", 1)
    stacked = pad_rows(jnp.concatenate([earlier, latent_wide], axis=0))
    extended = (conv_taps(stacked, in_weight, frames + 2, height, columns + 2) + in_bias).astype(
        jnp.bfloat16
    )
    extended = extended.reshape(frames + 2, height, columns + 2, half_channels)
    upblock_half = extended[2:, :, 1 : columns + 1]
    extended_full = lax.all_gather(extended, "tp", axis=3, tiled=True)
    normed = activate(extended_full, norm_gain)
    frame_index = lax.axis_index("sp") * frames - 2 + jnp.arange(frames + 2, dtype=jnp.int32)
    column_index = (
        lax.axis_index("section") * columns - 1 + jnp.arange(columns + 2, dtype=jnp.int32)
    )
    inside_cols = (column_index >= 0) & (column_index < columns * sections)
    inside = (frame_index >= 0)[:, None, None, None] & inside_cols[None, None, :, None]
    conv_input = pad_rows(jnp.where(inside, normed, jnp.zeros_like(normed)))
    full_weight = lax.all_gather(conv_weight, "section", axis=1, tiled=True)
    mixed = conv_taps(conv_input, full_weight, frames, height, columns)
    decoded = (
        upblock_half.astype(jnp.float32).reshape(-1, half_channels) + mixed + conv_bias
    ).astype(jnp.bfloat16)
    return decoded.reshape(frames, height, columns, half_channels)


def head_kernel(
    hidden_hbm, modulation_hbm, embed_hbm, weight_hbm, bias_hbm, place_hbm, shift_hbm,
    out, place, head_bias, hidden, modulation, time_embed, weight, in_bias, arrived, *, parts
):
    tokens, features = hidden.shape
    outs = weight.shape[0]
    wide = features // parts
    small = [
        pltpu.make_async_copy(source, target, arrived.at[i])
        for i, (source, target) in enumerate(
            ((modulation_hbm, modulation), (embed_hbm, time_embed), (bias_hbm, in_bias))
        )
    ]
    later = [
        pltpu.make_async_copy(source, target, arrived.at[3 + 2 * parts + i])
        for i, (source, target) in enumerate(((place_hbm, place), (shift_hbm, head_bias)))
    ]
    large = []
    for part in range(parts):
        cut = pl.ds(part * wide, wide)
        large.append(
            [
                pltpu.make_async_copy(
                    source.at[:, cut], target.at[:, cut], arrived.at[3 + 2 * part + i]
                )
                for i, (source, target) in enumerate(((hidden_hbm, hidden), (weight_hbm, weight)))
            ]
        )
    for copy in small + [copy for pair in large for copy in pair] + later:
        copy.start()
    for copy in small:
        copy.wait()
    sums, first, second = 0.0, 0.0, 0.0
    row = lax.broadcasted_iota(jnp.int32, (16, wide), 0)
    for part in range(parts):
        for copy in large[part]:
            copy.wait()
        cut = slice(part * wide, (part + 1) * wide)
        x = hidden[:, cut].astype(F32)
        embed = time_embed[:, cut]
        scale = 1.0 + (modulation[1:2, cut] + embed)
        shift = modulation[0:1, cut] + embed
        scaled = x * scale
        high = scaled.astype(BF16)
        low = (scaled - high.astype(F32)).astype(BF16)
        scale_high = scale.astype(BF16).astype(F32)
        shift_high = shift.astype(BF16).astype(F32)
        extra = jnp.where(row == 0, scale_high, 0.0)
        extra = jnp.where(row == 1, scale - scale_high, extra)
        extra = jnp.where(row == 2, shift_high, extra)
        extra = jnp.where(row == 3, shift - shift_high, extra).astype(BF16)
        stacked = jnp.concatenate([high, low, extra], axis=0)
        sums = sums + lax.dot_general(
            stacked, weight[:, cut], (((1,), (1,)), ((), ())), preferred_element_type=F32
        )
        first = first + jnp.sum(x, axis=1, keepdims=True)
        second = second + jnp.sum(x * x, axis=1, keepdims=True)
    out[0:tokens, 0:outs] = sums[0:tokens] + sums[tokens : 2 * tokens]
    lane = lax.broadcasted_iota(jnp.int32, (tokens, outs), 1)
    out[0:tokens, outs : 2 * outs] = jnp.where(lane == 0, first, second)
    base = 2 * tokens
    out[tokens : tokens + 1, 0:outs] = sums[base : base + 1] + sums[base + 1 : base + 2]
    out[tokens : tokens + 1, outs : 2 * outs] = sums[base + 2 : base + 3] + sums[base + 3 : base + 4]
    biases = in_bias.shape[0]
    out[tokens + 1 : tokens + 1 + biases, :] = in_bias[...]
    rest = out.shape[0] - tokens - 1 - biases
    out[tokens + 1 + biases :, :] = jnp.zeros((rest, out.shape[1]), F32)
    for copy in later:
        copy.wait()


def stage_kernel(_, *refs, scalar):
    arrived, refs = refs[-1], refs[:-1]
    if scalar:
        refs[-1][...] = jnp.full(refs[-1].shape, refs[0][0], F32)
        refs = refs[1:-1]
    count = len(refs) // 2
    copies = [
        pltpu.make_async_copy(source, target, arrived.at[i])
        for i, (source, target) in enumerate(zip(refs[:count], refs[count:], strict=True))
    ]
    for copy in copies:
        copy.start()
    for copy in copies:
        copy.wait()


def message_kernel(mine, other, bias, place, noisy, out, *, features, cells, channels):
    tokens, outs = place.shape[0], bias.shape[1]
    total = mine[...] + other[...]
    average = total[0:tokens, outs : outs + 1] / features
    variance = total[0:tokens, outs + 1 : outs + 2] / features - average * average
    inverse = lax.rsqrt(variance + 1e-06)
    scale_sum = total[tokens : tokens + 1, 0:outs]
    shift_sum = total[tokens : tokens + 1, outs : 2 * outs]
    velocity = inverse * (total[0:tokens, 0:outs] - average * scale_sum) + (shift_sum + bias[...])
    velocity = velocity.astype(BF16)
    spread = lax.dot_general(
        velocity, place[...], (((0,), (0,)), ((), ())), preferred_element_type=F32
    )
    field = spread[0:channels, 0:cells]
    for part in range(1, outs // channels):
        field = field + spread[
            part * channels : (part + 1) * channels, part * cells : (part + 1) * cells
        ]
    for target in range(out.shape[0]):
        out[target, :, 0:cells] = field.astype(BF16)
        out[target, :, cells:] = noisy[...]


def latents(messages, first, step, std, mean, sections, members, cells):
    lat = std.shape[1]
    diagonal = lax.broadcasted_iota(jnp.int32, (lat, lat), 0) == lax.broadcasted_iota(
        jnp.int32, (lat, lat), 1
    )
    deviation = jnp.sum(jnp.where(diagonal, std[...], 0.0), axis=1, keepdims=True)
    middle = jnp.sum(jnp.where(diagonal, mean[...], 0.0), axis=1, keepdims=True)
    parts = [messages[first + s * members].astype(F32) for s in range(sections)]
    tile = cells // sections
    frames = []
    for frame in range(sections):
        cut = slice(cells + frame * tile, cells + (frame + 1) * tile)
        noisy = jnp.concatenate([part[:, cut] for part in parts], axis=1)
        latent = (noisy - step * parts[frame][:, 0:cells]) * deviation + middle
        frames.append(latent.astype(BF16).astype(F32))
    return jnp.concatenate(frames, axis=1)


def conv_tile(normed, conv, first_column, columns, frames):
    height, deep = normed.shape[3:]
    taps, _, half = conv.shape
    size = frames * columns * height
    total = 0.0
    for first in range(0, taps, 2):
        group = range(first, min(first + 2, taps))
        window = jnp.concatenate(
            [
                normed[
                    t // 3 % 3, t // 9 : t // 9 + frames, pl.ds(first_column + t % 3, columns)
                ].reshape(size, deep)
                for t in group
            ],
            axis=1,
        )
        weight = conv[first : first + len(group)].reshape(len(group) * deep, half)
        total = total + jnp.dot(window, weight, preferred_element_type=F32)
    return total


def norm_kernel(
    step, messages, std, mean, weight_mine, weight_other, sums_mine, sums_other, gain, conv,
    partial, tile, normed, rolled, blocks, *, frames, height, width, tokens, k, sections, members
):
    mine, side, member = (lax.axis_index(axis) for axis in ("section", "tp", "sp"))
    first_frame = member * frames - 2
    cells = height * width
    lat = messages.shape[1]
    lanes = 2 * frames * cells
    half = weight_mine.shape[1]
    deep = gain.shape[2]
    columns = tile.shape[1] // height
    per_half = half // deep
    block = jnp.where((mine // per_half) == side, 0, per_half) + mine % per_half
    rest = (step[:, 0:1], std, mean, sections, members, cells)
    earlier = latents(messages, jnp.maximum(member - 1, 0), *rest)
    earlier = jnp.where(member > 0, earlier, 0.0)
    x = jnp.concatenate([earlier, latents(messages, member, *rest)], axis=1)
    position = lax.broadcasted_iota(jnp.int32, (1, lanes), 1)
    at_row = position % height
    at_column = (position // height) % width
    for b in range(3):
        for e in range(3):
            offset = (e - 1) * height + (b - 1)
            moved = x if offset == 0 else pltpu.roll(x, (-offset) % lanes, axis=1)
            row, column = at_row + (b - 1), at_column + (e - 1)
            inside = (row >= 0) & (row < height) & (column >= 0) & (column < width)
            moved = jnp.where(inside, moved, 0.0)
            first = (3 * b + e) * lat
            rolled[first : first + lat, :] = moved.astype(BF16)
    bias_rows = [
        source[tokens + 1 + i : tokens + 2 + i, :]
        for source in (sums_mine, sums_other)
        for i in range(per_half)
    ]
    gain_row = gain[mine]
    edge = lax.broadcasted_iota(jnp.int32, (cells, 1), 0) % height
    zero_column = jnp.zeros((height, deep), BF16)
    for frame in range(frames + 2):
        stacked = jnp.concatenate(
            [rolled[:, (frame + a) * cells : (frame + a + 1) * cells] for a in range(3)], axis=0
        )
        squares = jnp.zeros((cells, deep), F32)
        for which, weight in enumerate((weight_mine, weight_other)):
            product = lax.dot_general(
                stacked, weight[...], (((0,), (0,)), ((), ())), preferred_element_type=F32
            )
            for i in range(per_half):
                n = which * per_half + i
                piece = (product[:, i * deep : (i + 1) * deep] + bias_rows[n]).astype(BF16)
                blocks[n] = piece
                wide = piece.astype(F32)
                squares = squares + wide * wide
        mean = jnp.sum(squares, axis=1, keepdims=True) / (2 * half)
        inverse = lax.rsqrt(mean + 1e-06)
        value = blocks[block].astype(F32) * inverse * gain_row
        value = value / (1.0 + jnp.exp(-value))
        if frame < 2:
            value = jnp.where(first_frame + frame >= 0, value, 0.0)
        above = jnp.where(edge == 0, 0.0, pltpu.roll(value, 1, axis=0))
        below = jnp.where(edge == height - 1, 0.0, pltpu.roll(value, cells - 1, axis=0))
        for b, shifted in enumerate((above, value, below)):
            normed[b, frame, 1 : width + 1] = shifted.astype(BF16).reshape(width, height, deep)
            normed[b, frame, 0] = zero_column
            normed[b, frame, width + 1] = zero_column
        if frame >= 2:
            rows = pl.ds(pl.multiple_of(mine * (columns * height), columns * height), columns * height)
            for i in range(per_half):
                tile[frame - 2, :, i * deep : (i + 1) * deep] = blocks[i, rows, :]
    partial[...] = conv_tile(normed, conv, (mine ^ k) * columns, columns, frames).astype(BF16)


def tile_kernel(normed, conv, partial, *, columns, frames, k):
    partial[...] = conv_tile(normed, conv, (lax.axis_index("section") ^ k) * columns, columns, frames).astype(
        partial.dtype
    )


def finish_kernel(tile, bias, order, *refs):
    parts, out = refs[:-1], refs[-1]
    rows, (height, columns) = tile.shape[1], out.shape[1:3]
    for frame in range(tile.shape[0]):
        total = tile[frame].astype(F32) + bias[...]
        for part in parts:
            total = total + part[frame * rows : (frame + 1) * rows, :].astype(F32)
        placed = jnp.dot(order[...], total.astype(BF16), preferred_element_type=F32)
        out[frame] = placed.reshape(height, columns, -1).astype(BF16)


def vmem(count):
    return [pl.BlockSpec(memory_space=pltpu.VMEM)] * count


SMEM = pl.BlockSpec(memory_space=pltpu.SMEM)
HBM = pl.BlockSpec(memory_space=pltpu.HBM)


VMEM_LIMIT = 12 * 2**20


def call(kernel, shapes, in_specs, scratch=(), last=False):
    single = not isinstance(shapes, (list, tuple))
    specs = pl.BlockSpec(memory_space=pltpu.VMEM) if single else vmem(len(shapes))
    if not last:
        local = [pltpu.VMEM(s.shape, s.dtype) for s in ([shapes] if single else shapes)]
        shapes = local[0] if single else local
    run = pl.pallas_call(
        kernel, out_shape=shapes, in_specs=in_specs, out_specs=specs, scratch_shapes=list(scratch),
        compiler_params=pltpu.CompilerParams(vmem_limit_bytes=VMEM_LIMIT),
    )

    def constrained(*args):
        return run(
            *[
                arg if spec is SMEM else pltpu.with_memory_space_constraint(arg, spec.memory_space)
                for arg, spec in zip(args, in_specs, strict=True)
            ]
        )

    return constrained


def staged(after, *arrays, scalar=None):
    shapes = [jax.ShapeDtypeStruct(x.shape, x.dtype) for x in arrays]
    first, specs = [after], vmem(1)
    if scalar is not None:
        shapes.append(jax.ShapeDtypeStruct((1, 128), F32))
        first, specs = first + [scalar], specs + [SMEM]
    return call(
        lambda *refs: stage_kernel(*refs, scalar=scalar is not None), shapes,
        specs + [HBM] * len(arrays), [pltpu.SemaphoreType.DMA((len(arrays),))],
    )(*first, *arrays)


def token_places(height, width):
    cells = height * width
    table = np.zeros((cells // 4, 4, cells), np.float32)
    for i in range(height // 2):
        for j in range(width // 2):
            for p in range(2):
                for q in range(2):
                    cell = (2 * j + q) * height + 2 * i + p
                    table[i * (width // 2) + j, 2 * p + q, cell] = 1.0
    return table.reshape(cells // 4, 4 * cells)


def row_order(height, columns):
    table = np.zeros((height * columns, height * columns), np.float32)
    for h in range(height):
        for w in range(columns):
            table[h * columns + w, w * height + h] = 1.0
    return table


def send_order(sections):
    order = list(range(1, sections))
    return sorted(order, key=lambda k: (k == sections - 1, -k))


def sectioned_shards(
    hidden, modulation, time_embed, head_weight, head_bias, noisy, step_size,
    latent_mean, latent_std, in_weight, in_bias, norm_gain, conv_weight, conv_bias,
):
    frames, height, columns, lat = noisy.shape
    sections, halves = lax.axis_size("section"), lax.axis_size("tp")
    members = lax.axis_size("sp")
    width, half = columns * sections, in_weight.shape[2]
    cells = height * width
    tokens, local = hidden.shape
    outs = head_weight.shape[1]
    deep = conv_weight.shape[1]
    per_half = half // deep
    swap = [(i, i ^ 1) for i in range(halves)]
    taps = in_weight.shape[0]

    noisy_rows = jnp.transpose(noisy, (3, 0, 2, 1)).reshape(lat, frames * columns * height)
    parts = 3 if local % (3 * 128) == 0 else 1
    head_in = (
        hidden, modulation, time_embed.reshape(1, local), head_weight.T,
        in_bias.reshape(per_half, deep),
    )
    kept = (jnp.asarray(token_places(height, width), BF16), head_bias.reshape(1, outs))
    sums, place, head_bias = call(
        lambda *refs: head_kernel(*refs, parts=parts),
        [jax.ShapeDtypeStruct((tokens + 8, 2 * outs), F32)]
        + [jax.ShapeDtypeStruct(x.shape, x.dtype) for x in kept],
        [HBM] * (len(head_in) + len(kept)),
        [pltpu.VMEM(x.shape, x.dtype) for x in head_in]
        + [pltpu.SemaphoreType.DMA((5 + 2 * parts,))],
    )(*head_in, *kept)
    sums_other = lax.ppermute(sums, "tp", swap)
    message = call(
        lambda *refs: message_kernel(
            *refs, features=local * halves, cells=cells, channels=lat
        ),
        jax.ShapeDtypeStruct((sections * members, lat, 2 * cells), BF16), vmem(5),
    )(sums, sums_other, head_bias, place, noisy_rows)
    messages = lax.all_to_all(message, ("section", "sp"), 0, 0)
    latent_std, latent_mean, conv, weight_mine, gain, order, conv_bias, step = staged(
        message, latent_std.reshape(1, lat), latent_mean.reshape(1, lat),
        conv_weight, in_weight.reshape(taps * lat, half),
        norm_gain.reshape(sections, 1, deep), jnp.asarray(row_order(height, columns), BF16),
        conv_bias.reshape(1, half), scalar=step_size,
    )
    weight_other = lax.ppermute(weight_mine, "tp", swap)

    size = frames * columns * height
    sends = send_order(sections)
    partials = {}
    partials[sends[0]], tile, normed = call(
        lambda *refs: norm_kernel(
            *refs, frames=frames, height=height, width=width, tokens=tokens, k=sends[0],
            sections=sections, members=members
        ),
        [
            jax.ShapeDtypeStruct((size, half), BF16),
            jax.ShapeDtypeStruct((frames, columns * height, half), BF16),
            jax.ShapeDtypeStruct((3, frames + 2, width + 2, height, deep), BF16),
        ],
        vmem(10),
        [
            pltpu.VMEM((9 * lat, 2 * frames * cells), BF16),
            pltpu.VMEM((sections, cells, deep), BF16),
        ],
    )(
        step, messages, latent_std, latent_mean, weight_mine, weight_other, sums,
        sums_other, gain, conv,
    )
    received = {}
    for k in sends + [0]:
        if k not in partials:
            partials[k] = call(
                lambda *refs: tile_kernel(*refs, columns=columns, frames=frames, k=k),
                jax.ShapeDtypeStruct((size, half), BF16 if k else F32), vmem(2),
            )(normed, conv)
        if k:
            received[k] = lax.ppermute(
                partials[k], "section", [(i, i ^ k) for i in range(sections)]
            )
    return call(
        finish_kernel, jax.ShapeDtypeStruct((frames, height, columns, half), BF16),
        vmem(3 + sections), last=True,
    )(tile, conv_bias, order, partials[0], *[received[k] for k in sends])


def sectioned(mesh):
    def fits(hidden, head_weight, noisy, in_weight, conv_weight):
        frames, height, columns, _ = noisy.shape
        sections = mesh.shape["section"]
        cells = height * columns * sections
        deep = conv_weight.shape[1]
        return (
            sections == frames
            and sections & (sections - 1) == 0
            and hidden.shape[0] * 4 == cells
            and mesh.shape["tp"] == 2
            and in_weight.shape[2] == 2 * deep
            and 2 * in_weight.shape[2] == sections * deep
            and deep % 128 == 0
            and 2 * head_weight.shape[1] == deep
            and height % 16 == 0
            and cells % 128 == 0
        )

    return fits


def solution(mesh):
    placed = (
        P(("groups", "sp", "section"), "tp"),
        P(None, "tp"),
        P(("groups", "tp")),
        P("tp", None),
        P(),
        P(("groups", "sp"), None, "section", None),
        P("groups"),
        P(),
        P(),
        P(None, None, "tp"),
        P("tp"),
        P(),
        P(None, "section", "tp"),
        P("tp"),
    )
    fits = sectioned(mesh)

    def shards(*args):
        if not fits(args[0], args[3], args[5], args[9], args[12]):
            return general_shards(*args)
        return sectioned_shards(*args)

    return jax.shard_map(
        shards,
        mesh=mesh,
        in_specs=placed,
        out_specs=P(("groups", "sp"), None, "section", "tp"),
        check_vma=False,
    )
```

```python
import jax
import jax.numpy as jnp
import numpy as np
from jax import lax
from jax.experimental import pallas as pl
from jax.experimental.pallas import tpu as pltpu
from jax.sharding import PartitionSpec as P

F32 = jnp.float32
BF16 = jnp.bfloat16


def padded_2(value, sides, width):
    for axis, dim in sides:
        count, length = (lax.axis_size(axis), value.shape[dim])
        up = [(i, (i + 1) % count) for i in range(count - 1)]
        down = [(j, i) for i, j in up]
        last = lax.slice_in_dim(value, length - width, length, axis=dim)
        leading = lax.slice_in_dim(value, 0, width, axis=dim)
        before = lax.ppermute(last, axis, up)
        after = lax.ppermute(leading, axis, down)
        value = jnp.concatenate([before, value, after], axis=dim)
    return value


def passed_along(value, axis, by):
    count = lax.axis_size(axis)
    pairs = [(i, i + by) for i in range(count) if 0 <= i + by < count]
    return lax.ppermute(value, axis, pairs)


def conv_taps(padded, weight, frames, height, columns):
    channels = padded.shape[3]
    result = jnp.zeros((frames * height * columns, weight.shape[2]), jnp.float32)
    for offset_time in range(3):
        for offset_row in range(3):
            slab = padded[offset_time : offset_time + frames, offset_row : offset_row + height]
            window = jnp.concatenate(
                [slab[:, :, 0:columns], slab[:, :, 1 : columns + 1], slab[:, :, 2 : columns + 2]],
                axis=3,
            )
            first = 9 * offset_time + 3 * offset_row
            taps = weight[first : first + 3].reshape(3 * channels, weight.shape[2])
            result = result + jnp.dot(
                window.reshape(-1, 3 * channels), taps, preferred_element_type=jnp.float32
            )
    return result


def activate(source, gain_vector):
    values = source.astype(jnp.float32)
    squares = jnp.mean(values * values, axis=-1, keepdims=True)
    return jax.nn.silu(values * lax.rsqrt(squares + 1e-06) * gain_vector).astype(jnp.bfloat16)


def pad_rows(source):
    return jnp.pad(source, ((0, 0), (1, 1), (0, 0), (0, 0)))


def general_shards(
    hidden, modulation, time_embed, head_weight, head_bias, noisy, step_size,
    latent_mean, latent_std, in_weight, in_bias, norm_gain, conv_weight, conv_bias,
):
    frames, height, columns, lat_channels = noisy.shape
    sections = lax.axis_size("section")
    half_channels = in_weight.shape[2]
    features = hidden.shape[1] * lax.axis_size("tp")
    values = hidden.astype(jnp.float32)
    row_sums, square_sums = lax.psum(
        (jnp.sum(values, axis=1), jnp.sum(values * values, axis=1)), "tp"
    )
    average = row_sums / features
    variance = square_sums / features - average * average
    shift_term = modulation[0] + time_embed
    scale_term = modulation[1] + time_embed
    modulated = (
        (values - average[:, None]) * lax.rsqrt(variance[:, None] + 1e-06) * (1.0 + scale_term)
        + shift_term
    ).astype(jnp.bfloat16)
    partial_sum = jnp.dot(modulated, head_weight, preferred_element_type=jnp.float32)
    velocity = (lax.psum(partial_sum, "tp") + head_bias).astype(jnp.bfloat16)
    band_rows = velocity.shape[0] * 2 // (columns * sections)
    outgoing = velocity.reshape(band_rows, sections, -1)
    arrived = lax.all_to_all(outgoing, "section", split_axis=1, concat_axis=0, tiled=True)
    latent_field = arrived.reshape(frames, height // 2, columns // 2, 2, 2, lat_channels)
    latent_field = jnp.transpose(latent_field, (0, 1, 3, 2, 4, 5)).reshape(
        frames, height, columns, lat_channels
    )
    latent = (
        (noisy.astype(jnp.float32) - step_size[0] * latent_field.astype(jnp.float32)) * latent_std
        + latent_mean
    ).astype(jnp.bfloat16)
    latent_wide = padded_2(latent, (("section", 2),), 2)
    earlier = passed_along(latent_wide, "sp", 1)
    stacked = pad_rows(jnp.concatenate([earlier, latent_wide], axis=0))
    extended = (conv_taps(stacked, in_weight, frames + 2, height, columns + 2) + in_bias).astype(
        jnp.bfloat16
    )
    extended = extended.reshape(frames + 2, height, columns + 2, half_channels)
    upblock_half = extended[2:, :, 1 : columns + 1]
    extended_full = lax.all_gather(extended, "tp", axis=3, tiled=True)
    normed = activate(extended_full, norm_gain)
    frame_index = lax.axis_index("sp") * frames - 2 + jnp.arange(frames + 2, dtype=jnp.int32)
    column_index = (
        lax.axis_index("section") * columns - 1 + jnp.arange(columns + 2, dtype=jnp.int32)
    )
    inside_cols = (column_index >= 0) & (column_index < columns * sections)
    inside = (frame_index >= 0)[:, None, None, None] & inside_cols[None, None, :, None]
    conv_input = pad_rows(jnp.where(inside, normed, jnp.zeros_like(normed)))
    full_weight = lax.all_gather(conv_weight, "section", axis=1, tiled=True)
    mixed = conv_taps(conv_input, full_weight, frames, height, columns)
    decoded = (
        upblock_half.astype(jnp.float32).reshape(-1, half_channels) + mixed + conv_bias
    ).astype(jnp.bfloat16)
    return decoded.reshape(frames, height, columns, half_channels)


def head_kernel(
    hidden_hbm, modulation_hbm, embed_hbm, weight_hbm, noisy_hbm, place_hbm, bias_hbm,
    out, rows, place, bias, hidden, modulation, time_embed, weight, noisy, arrived, *, parts
):
    tokens, features = hidden.shape
    outs = weight.shape[0]
    wide = features // parts
    small = [
        pltpu.make_async_copy(source, target, arrived.at[i])
        for i, (source, target) in enumerate(
            ((noisy_hbm, noisy), (modulation_hbm, modulation), (embed_hbm, time_embed))
        )
    ]
    later = [
        pltpu.make_async_copy(source, target, arrived.at[3 + 2 * parts + i])
        for i, (source, target) in enumerate(((place_hbm, place), (bias_hbm, bias)))
    ]
    large = []
    for part in range(parts):
        cut = pl.ds(part * wide, wide)
        large.append(
            [
                pltpu.make_async_copy(
                    source.at[:, cut], target.at[:, cut], arrived.at[3 + 2 * part + i]
                )
                for i, (source, target) in enumerate(((hidden_hbm, hidden), (weight_hbm, weight)))
            ]
        )
    for copy in small + [copy for pair in large for copy in pair] + later:
        copy.start()
    for copy in small:
        copy.wait()
    cells = noisy[...].astype(F32)
    rows[...] = jnp.concatenate(
        [cells[f, :, w, :] for f in range(cells.shape[0]) for w in range(cells.shape[2])], axis=0
    ).T.astype(BF16)
    sums, first, second = 0.0, 0.0, 0.0
    row = lax.broadcasted_iota(jnp.int32, (16, wide), 0)
    for part in range(parts):
        for copy in large[part]:
            copy.wait()
        cut = slice(part * wide, (part + 1) * wide)
        x = hidden[:, cut].astype(F32)
        embed = time_embed[:, cut]
        scale = 1.0 + (modulation[1:2, cut] + embed)
        shift = modulation[0:1, cut] + embed
        scaled = x * scale
        high = scaled.astype(BF16)
        low = (scaled - high.astype(F32)).astype(BF16)
        scale_high = scale.astype(BF16).astype(F32)
        shift_high = shift.astype(BF16).astype(F32)
        extra = jnp.where(row == 0, scale_high, 0.0)
        extra = jnp.where(row == 1, scale - scale_high, extra)
        extra = jnp.where(row == 2, shift_high, extra)
        extra = jnp.where(row == 3, shift - shift_high, extra).astype(BF16)
        stacked = jnp.concatenate([high, low, extra], axis=0)
        sums = sums + lax.dot_general(
            stacked, weight[:, cut], (((1,), (1,)), ((), ())), preferred_element_type=F32
        )
        first = first + jnp.sum(x, axis=1, keepdims=True)
        second = second + jnp.sum(x * x, axis=1, keepdims=True)
    out[0:tokens, 0:outs] = sums[0:tokens] + sums[tokens : 2 * tokens]
    lane = lax.broadcasted_iota(jnp.int32, (tokens, outs), 1)
    out[0:tokens, outs : 2 * outs] = jnp.where(lane == 0, first, second)
    base = 2 * tokens
    out[tokens : tokens + 1, 0:outs] = sums[base : base + 1] + sums[base + 1 : base + 2]
    out[tokens : tokens + 1, outs : 2 * outs] = sums[base + 2 : base + 3] + sums[base + 3 : base + 4]
    out[tokens + 1 :, :] = jnp.zeros((out.shape[0] - tokens - 1, out.shape[1]), F32)
    for copy in later:
        copy.wait()


def stage_kernel(_, step, weight_hbm, bias_hbm, *refs):
    bias, arrived, refs = refs[-2], refs[-1], refs[:-2]
    count = len(refs) // 2 - 1
    step_row, weight = refs[count : count + 2]
    taps = weight_hbm.shape[0]
    pairs = [(weight_hbm, weight.at[0:taps]), (bias_hbm, bias)]
    pairs += list(zip(refs[:count], refs[count + 2 :], strict=True))
    copies = [
        pltpu.make_async_copy(source, target, arrived.at[i])
        for i, (source, target) in enumerate(pairs)
    ]
    for copy in copies:
        copy.start()
    step_row[...] = jnp.full(step_row.shape, step[0], F32)
    copies[1].wait()
    rest, below = bias[...], weight.shape[0] - taps
    row = lax.broadcasted_iota(jnp.int32, (below, rest.shape[1]), 0)
    rows = jnp.zeros(row.shape, F32)
    for part in range(3):
        piece = rest.astype(BF16).astype(F32)
        rows = jnp.where(row == part, piece, rows)
        rest = rest - piece
    weight[taps:] = rows.astype(BF16)
    for i, copy in enumerate(copies):
        if i != 1:
            copy.wait()


def message_kernel(mine, other, bias, place, noisy, out, *, features, cells, channels):
    tokens, outs = place.shape[0], bias.shape[1]
    total = mine[...] + other[...]
    average = total[0:tokens, outs : outs + 1] / features
    variance = total[0:tokens, outs + 1 : outs + 2] / features - average * average
    inverse = lax.rsqrt(variance + 1e-06)
    scale_sum = total[tokens : tokens + 1, 0:outs]
    shift_sum = total[tokens : tokens + 1, outs : 2 * outs]
    velocity = inverse * (total[0:tokens, 0:outs] - average * scale_sum) + (shift_sum + bias[...])
    velocity = velocity.astype(BF16)
    spread = lax.dot_general(
        velocity, place[...], (((0,), (0,)), ((), ())), preferred_element_type=F32
    )
    field = spread[0:channels, 0:cells]
    for part in range(1, outs // channels):
        field = field + spread[
            part * channels : (part + 1) * channels, part * cells : (part + 1) * cells
        ]
    for target in range(out.shape[0]):
        out[target, :, 0:cells] = field.astype(BF16)
        out[target, :, cells:] = noisy[...]


def latents(messages, first, step, std, mean, sections, members, cells):
    lat = std.shape[1]
    diagonal = lax.broadcasted_iota(jnp.int32, (lat, lat), 0) == lax.broadcasted_iota(
        jnp.int32, (lat, lat), 1
    )
    deviation = jnp.sum(jnp.where(diagonal, std[...], 0.0), axis=1, keepdims=True)
    middle = jnp.sum(jnp.where(diagonal, mean[...], 0.0), axis=1, keepdims=True)
    parts = [messages[first + s * members].astype(F32) for s in range(sections)]
    tile = cells // sections
    frames = []
    for frame in range(sections):
        cut = slice(cells + frame * tile, cells + (frame + 1) * tile)
        noisy = jnp.concatenate([part[:, cut] for part in parts], axis=1)
        latent = (noisy - step * parts[frame][:, 0:cells]) * deviation + middle
        frames.append(latent.astype(BF16).astype(F32))
    return jnp.concatenate(frames, axis=1)


def conv_tile(normed, conv, first_column, columns, frames):
    height, deep = normed.shape[3:]
    taps, _, half = conv.shape
    size = frames * columns * height
    total = 0.0
    for first in range(0, taps, 2):
        group = range(first, min(first + 2, taps))
        window = jnp.concatenate(
            [
                normed[
                    t // 3 % 3, t // 9 : t // 9 + frames, pl.ds(first_column + t % 3, columns)
                ].reshape(size, deep)
                for t in group
            ],
            axis=1,
        )
        weight = conv[first : first + len(group)].reshape(len(group) * deep, half)
        total = total + jnp.dot(window, weight, preferred_element_type=F32)
    return total


def norm_kernel(
    step, messages, std, mean, weight_mine, weight_other, gain, conv,
    partial, tile, normed, rolled, own, *, frames, height, width, k, sections, members
):
    mine, side, member = (lax.axis_index(axis) for axis in ("section", "tp", "sp"))
    first_frame = member * frames - 2
    cells = height * width
    lat = messages.shape[1]
    lanes = 2 * frames * cells
    half = weight_mine.shape[1]
    deep = gain.shape[2]
    columns = tile.shape[1] // height
    per_half = half // deep
    block = jnp.where((mine // per_half) == side, 0, per_half) + mine % per_half
    rest = (step[:, 0:1], std, mean, sections, members, cells)
    earlier = latents(messages, jnp.maximum(member - 1, 0), *rest)
    earlier = jnp.where(member > 0, earlier, 0.0)
    x = jnp.concatenate([earlier, latents(messages, member, *rest)], axis=1)
    position = lax.broadcasted_iota(jnp.int32, (1, lanes), 1)
    at_row = position % height
    at_column = (position // height) % width
    for b in range(3):
        for e in range(3):
            offset = (e - 1) * height + (b - 1)
            moved = x if offset == 0 else pltpu.roll(x, (-offset) % lanes, axis=1)
            row, column = at_row + (b - 1), at_column + (e - 1)
            inside = (row >= 0) & (row < height) & (column >= 0) & (column < width)
            moved = jnp.where(inside, moved, 0.0)
            first = (3 * b + e) * lat
            rolled[first : first + lat, :] = moved.astype(BF16)
    ones = jnp.ones((weight_mine.shape[0] - 27 * lat, cells), BF16)
    half_gain = 0.5 * gain[mine]
    edge = lax.broadcasted_iota(jnp.int32, (cells, 1), 0) % height
    zero_column = jnp.zeros((height, deep), BF16)
    for frame in range(frames + 2):
        stacked = jnp.concatenate(
            [rolled[:, (frame + a) * cells : (frame + a + 1) * cells] for a in range(3)] + [ones],
            axis=0,
        )
        squares, chosen = 0.0, 0.0
        for which, weight in enumerate((weight_mine, weight_other)):
            product = lax.dot_general(
                stacked, weight[...], (((0,), (0,)), ((), ())), preferred_element_type=F32
            )
            for i in range(per_half):
                piece = product[:, i * deep : (i + 1) * deep]
                squares = squares + piece * piece
                chosen = jnp.where(block == which * per_half + i, piece, chosen)
            if frame >= 2 and which == 0:
                own[frame - 2] = product.astype(BF16)
        mean = jnp.sum(squares, axis=1, keepdims=True) / (2 * half)
        value = chosen.astype(BF16).astype(F32) * lax.rsqrt(mean + 1e-06) * half_gain
        value = value * (1.0 + jnp.tanh(value))
        if frame < 2:
            value = jnp.where(first_frame + frame >= 0, value, 0.0)
        above = jnp.where(edge == 0, 0.0, pltpu.roll(value, 1, axis=0))
        below = jnp.where(edge == height - 1, 0.0, pltpu.roll(value, cells - 1, axis=0))
        for b, shifted in enumerate((above, value, below)):
            normed[b, frame, 1 : width + 1] = shifted.astype(BF16).reshape(width, height, deep)
            normed[b, frame, 0] = zero_column
            normed[b, frame, width + 1] = zero_column
    rows = pl.ds(pl.multiple_of(mine * (columns * height), columns * height), columns * height)
    for frame in range(frames):
        tile[frame] = own[frame, rows, :]
    partial[...] = conv_tile(normed, conv, (mine ^ k) * columns, columns, frames).astype(BF16)


def tile_kernel(normed, conv, partial, *, columns, frames, k):
    partial[...] = conv_tile(normed, conv, (lax.axis_index("section") ^ k) * columns, columns, frames).astype(
        partial.dtype
    )


def finish_kernel(tile, bias, order, *refs):
    parts, out = refs[:-1], refs[-1]
    rows, (height, columns) = tile.shape[1], out.shape[1:3]
    for frame in range(tile.shape[0]):
        total = tile[frame].astype(F32) + bias[...]
        for part in parts:
            total = total + part[frame * rows : (frame + 1) * rows, :].astype(F32)
        placed = jnp.dot(order[...], total.astype(BF16), preferred_element_type=F32)
        out[frame] = placed.reshape(height, columns, -1).astype(BF16)


def vmem(count):
    return [pl.BlockSpec(memory_space=pltpu.VMEM)] * count


SMEM = pl.BlockSpec(memory_space=pltpu.SMEM)
HBM = pl.BlockSpec(memory_space=pltpu.HBM)


VMEM_LIMIT = 12 * 2**20


def call(kernel, shapes, in_specs, scratch=(), last=False):
    single = not isinstance(shapes, (list, tuple))
    specs = pl.BlockSpec(memory_space=pltpu.VMEM) if single else vmem(len(shapes))
    if not last:
        local = [pltpu.VMEM(s.shape, s.dtype) for s in ([shapes] if single else shapes)]
        shapes = local[0] if single else local
    run = pl.pallas_call(
        kernel, out_shape=shapes, in_specs=in_specs, out_specs=specs, scratch_shapes=list(scratch),
        compiler_params=pltpu.CompilerParams(vmem_limit_bytes=VMEM_LIMIT),
    )

    def constrained(*args):
        return run(
            *[
                arg if spec is SMEM else pltpu.with_memory_space_constraint(arg, spec.memory_space)
                for arg, spec in zip(args, in_specs, strict=True)
            ]
        )

    return constrained


def staged(after, step, weight, bias, *arrays):
    shapes = [
        jax.ShapeDtypeStruct((1, 128), F32),
        jax.ShapeDtypeStruct((weight.shape[0] + 16, weight.shape[1]), weight.dtype),
    ]
    shapes += [jax.ShapeDtypeStruct(x.shape, x.dtype) for x in arrays]
    return call(
        stage_kernel, shapes, vmem(1) + [SMEM] + [HBM] * (2 + len(arrays)),
        [pltpu.VMEM(bias.shape, F32), pltpu.SemaphoreType.DMA((2 + len(arrays),))],
    )(after, step, weight, bias, *arrays)


def token_places(height, width):
    cells = height * width
    table = np.zeros((cells // 4, 4, cells), np.float32)
    for i in range(height // 2):
        for j in range(width // 2):
            for p in range(2):
                for q in range(2):
                    cell = (2 * j + q) * height + 2 * i + p
                    table[i * (width // 2) + j, 2 * p + q, cell] = 1.0
    return table.reshape(cells // 4, 4 * cells)


def row_order(height, columns):
    table = np.zeros((height * columns, height * columns), np.float32)
    for h in range(height):
        for w in range(columns):
            table[h * columns + w, w * height + h] = 1.0
    return table


def send_order(sections):
    order = list(range(1, sections))
    return sorted(order, key=lambda k: (k == sections - 1, -k))


def sectioned_shards(
    hidden, modulation, time_embed, head_weight, head_bias, noisy, step_size,
    latent_mean, latent_std, in_weight, in_bias, norm_gain, conv_weight, conv_bias,
):
    frames, height, columns, lat = noisy.shape
    sections, halves = lax.axis_size("section"), lax.axis_size("tp")
    members = lax.axis_size("sp")
    width, half = columns * sections, in_weight.shape[2]
    cells = height * width
    tokens, local = hidden.shape
    outs = head_weight.shape[1]
    deep = conv_weight.shape[1]
    swap = [(i, i ^ 1) for i in range(halves)]
    taps = in_weight.shape[0]

    parts = 3 if local % (3 * 128) == 0 else 1
    head_in = (
        hidden, modulation, time_embed.reshape(1, local), head_weight.T, noisy,
    )
    kept = (jnp.asarray(token_places(height, width), BF16), head_bias.reshape(1, outs))
    sums, noisy_rows, place, head_bias = call(
        lambda *refs: head_kernel(*refs, parts=parts),
        [
            jax.ShapeDtypeStruct((tokens + 8, 2 * outs), F32),
            jax.ShapeDtypeStruct((lat, frames * columns * height), BF16),
        ]
        + [jax.ShapeDtypeStruct(x.shape, x.dtype) for x in kept],
        [HBM] * (len(head_in) + len(kept)),
        [pltpu.VMEM(x.shape, x.dtype) for x in head_in]
        + [pltpu.SemaphoreType.DMA((5 + 2 * parts,))],
    )(*head_in, *kept)
    sums_other = lax.ppermute(sums, "tp", swap)
    message = call(
        lambda *refs: message_kernel(
            *refs, features=local * halves, cells=cells, channels=lat
        ),
        jax.ShapeDtypeStruct((sections * members, lat, 2 * cells), BF16), vmem(5),
    )(sums, sums_other, head_bias, place, noisy_rows)
    messages = lax.all_to_all(message, ("section", "sp"), 0, 0)
    step, weight_mine, latent_std, latent_mean, conv, gain, order, conv_bias = staged(
        message, step_size, in_weight.reshape(taps * lat, half), in_bias.reshape(1, half),
        latent_std.reshape(1, lat), latent_mean.reshape(1, lat), conv_weight,
        norm_gain.reshape(sections, 1, deep), jnp.asarray(row_order(height, columns), BF16),
        conv_bias.reshape(1, half),
    )
    weight_other = lax.ppermute(weight_mine, "tp", swap)

    size = frames * columns * height
    sends = send_order(sections)
    partials = {}
    partials[sends[0]], tile, normed = call(
        lambda *refs: norm_kernel(
            *refs, frames=frames, height=height, width=width, k=sends[0],
            sections=sections, members=members
        ),
        [
            jax.ShapeDtypeStruct((size, half), BF16),
            jax.ShapeDtypeStruct((frames, columns * height, half), BF16),
            jax.ShapeDtypeStruct((3, frames + 2, width + 2, height, deep), BF16),
        ],
        vmem(8),
        [
            pltpu.VMEM((9 * lat, 2 * frames * cells), BF16),
            pltpu.VMEM((frames, cells, half), BF16),
        ],
    )(
        step, messages, latent_std, latent_mean, weight_mine, weight_other, gain, conv,
    )
    received = {}
    for k in sends + [0]:
        if k not in partials:
            partials[k] = call(
                lambda *refs: tile_kernel(*refs, columns=columns, frames=frames, k=k),
                jax.ShapeDtypeStruct((size, half), BF16 if k else F32), vmem(2),
            )(normed, conv)
        if k:
            received[k] = lax.ppermute(
                partials[k], "section", [(i, i ^ k) for i in range(sections)]
            )
    return call(
        finish_kernel, jax.ShapeDtypeStruct((frames, height, columns, half), BF16),
        vmem(3 + sections), last=True,
    )(tile, conv_bias, order, partials[0], *[received[k] for k in sends])


def sectioned(mesh):
    def fits(hidden, head_weight, noisy, in_weight, conv_weight):
        frames, height, columns, _ = noisy.shape
        sections = mesh.shape["section"]
        cells = height * columns * sections
        deep = conv_weight.shape[1]
        return (
            sections == frames
            and sections & (sections - 1) == 0
            and hidden.shape[0] * 4 == cells
            and mesh.shape["tp"] == 2
            and in_weight.shape[2] == 2 * deep
            and 2 * in_weight.shape[2] == sections * deep
            and deep % 128 == 0
            and 2 * head_weight.shape[1] == deep
            and height % 16 == 0
            and cells % 128 == 0
        )

    return fits


def solution(mesh):
    placed = (
        P(("groups", "sp", "section"), "tp"),
        P(None, "tp"),
        P(("groups", "tp")),
        P("tp", None),
        P(),
        P(("groups", "sp"), None, "section", None),
        P("groups"),
        P(),
        P(),
        P(None, None, "tp"),
        P("tp"),
        P(),
        P(None, "section", "tp"),
        P("tp"),
    )
    fits = sectioned(mesh)

    def shards(*args):
        if not fits(args[0], args[3], args[5], args[9], args[12]):
            return general_shards(*args)
        return sectioned_shards(*args)

    return jax.shard_map(
        shards,
        mesh=mesh,
        in_specs=placed,
        out_specs=P(("groups", "sp"), None, "section", "tp"),
        check_vma=False,
    )
```

```python
import jax
import jax.numpy as jnp
import numpy as np
from jax import lax
from jax.experimental import pallas as pl
from jax.experimental.pallas import tpu as pltpu
from jax.sharding import PartitionSpec as P

F32 = jnp.float32
BF16 = jnp.bfloat16


def padded_2(value, sides, width):
    for axis, dim in sides:
        count, length = (lax.axis_size(axis), value.shape[dim])
        up = [(i, (i + 1) % count) for i in range(count - 1)]
        down = [(j, i) for i, j in up]
        last = lax.slice_in_dim(value, length - width, length, axis=dim)
        leading = lax.slice_in_dim(value, 0, width, axis=dim)
        before = lax.ppermute(last, axis, up)
        after = lax.ppermute(leading, axis, down)
        value = jnp.concatenate([before, value, after], axis=dim)
    return value


def passed_along(value, axis, by):
    count = lax.axis_size(axis)
    pairs = [(i, i + by) for i in range(count) if 0 <= i + by < count]
    return lax.ppermute(value, axis, pairs)


def conv_taps(padded, weight, frames, height, columns):
    channels = padded.shape[3]
    result = jnp.zeros((frames * height * columns, weight.shape[2]), jnp.float32)
    for offset_time in range(3):
        for offset_row in range(3):
            slab = padded[offset_time : offset_time + frames, offset_row : offset_row + height]
            window = jnp.concatenate(
                [slab[:, :, 0:columns], slab[:, :, 1 : columns + 1], slab[:, :, 2 : columns + 2]],
                axis=3,
            )
            first = 9 * offset_time + 3 * offset_row
            taps = weight[first : first + 3].reshape(3 * channels, weight.shape[2])
            result = result + jnp.dot(
                window.reshape(-1, 3 * channels), taps, preferred_element_type=jnp.float32
            )
    return result


def activate(source, gain_vector):
    values = source.astype(jnp.float32)
    squares = jnp.mean(values * values, axis=-1, keepdims=True)
    return jax.nn.silu(values * lax.rsqrt(squares + 1e-06) * gain_vector).astype(jnp.bfloat16)


def pad_rows(source):
    return jnp.pad(source, ((0, 0), (1, 1), (0, 0), (0, 0)))


def general_shards(
    hidden, modulation, time_embed, head_weight, head_bias, noisy, step_size,
    latent_mean, latent_std, in_weight, in_bias, norm_gain, conv_weight, conv_bias,
):
    frames, height, columns, lat_channels = noisy.shape
    sections = lax.axis_size("section")
    half_channels = in_weight.shape[2]
    features = hidden.shape[1] * lax.axis_size("tp")
    values = hidden.astype(jnp.float32)
    row_sums, square_sums = lax.psum(
        (jnp.sum(values, axis=1), jnp.sum(values * values, axis=1)), "tp"
    )
    average = row_sums / features
    variance = square_sums / features - average * average
    shift_term = modulation[0] + time_embed
    scale_term = modulation[1] + time_embed
    modulated = (
        (values - average[:, None]) * lax.rsqrt(variance[:, None] + 1e-06) * (1.0 + scale_term)
        + shift_term
    ).astype(jnp.bfloat16)
    partial_sum = jnp.dot(modulated, head_weight, preferred_element_type=jnp.float32)
    velocity = (lax.psum(partial_sum, "tp") + head_bias).astype(jnp.bfloat16)
    band_rows = velocity.shape[0] * 2 // (columns * sections)
    outgoing = velocity.reshape(band_rows, sections, -1)
    arrived = lax.all_to_all(outgoing, "section", split_axis=1, concat_axis=0, tiled=True)
    latent_field = arrived.reshape(frames, height // 2, columns // 2, 2, 2, lat_channels)
    latent_field = jnp.transpose(latent_field, (0, 1, 3, 2, 4, 5)).reshape(
        frames, height, columns, lat_channels
    )
    latent = (
        (noisy.astype(jnp.float32) - step_size[0] * latent_field.astype(jnp.float32)) * latent_std
        + latent_mean
    ).astype(jnp.bfloat16)
    latent_wide = padded_2(latent, (("section", 2),), 2)
    earlier = passed_along(latent_wide, "sp", 1)
    stacked = pad_rows(jnp.concatenate([earlier, latent_wide], axis=0))
    extended = (conv_taps(stacked, in_weight, frames + 2, height, columns + 2) + in_bias).astype(
        jnp.bfloat16
    )
    extended = extended.reshape(frames + 2, height, columns + 2, half_channels)
    upblock_half = extended[2:, :, 1 : columns + 1]
    extended_full = lax.all_gather(extended, "tp", axis=3, tiled=True)
    normed = activate(extended_full, norm_gain)
    frame_index = lax.axis_index("sp") * frames - 2 + jnp.arange(frames + 2, dtype=jnp.int32)
    column_index = (
        lax.axis_index("section") * columns - 1 + jnp.arange(columns + 2, dtype=jnp.int32)
    )
    inside_cols = (column_index >= 0) & (column_index < columns * sections)
    inside = (frame_index >= 0)[:, None, None, None] & inside_cols[None, None, :, None]
    conv_input = pad_rows(jnp.where(inside, normed, jnp.zeros_like(normed)))
    full_weight = lax.all_gather(conv_weight, "section", axis=1, tiled=True)
    mixed = conv_taps(conv_input, full_weight, frames, height, columns)
    decoded = (
        upblock_half.astype(jnp.float32).reshape(-1, half_channels) + mixed + conv_bias
    ).astype(jnp.bfloat16)
    return decoded.reshape(frames, height, columns, half_channels)


def head_kernel(
    hidden_hbm, modulation_hbm, embed_hbm, weight_hbm, noisy_hbm, place_hbm, bias_hbm,
    out, rows, place, bias, hidden, modulation, time_embed, weight, noisy, arrived, *, parts
):
    tokens, features = hidden.shape
    outs = weight.shape[0]
    wide = features // parts
    small = [
        pltpu.make_async_copy(source, target, arrived.at[i])
        for i, (source, target) in enumerate(
            ((noisy_hbm, noisy), (modulation_hbm, modulation), (embed_hbm, time_embed))
        )
    ]
    later = [
        pltpu.make_async_copy(source, target, arrived.at[3 + 2 * parts + i])
        for i, (source, target) in enumerate(((place_hbm, place), (bias_hbm, bias)))
    ]
    large = []
    for part in range(parts):
        cut = pl.ds(part * wide, wide)
        large.append(
            [
                pltpu.make_async_copy(
                    source.at[:, cut], target.at[:, cut], arrived.at[3 + 2 * part + i]
                )
                for i, (source, target) in enumerate(((hidden_hbm, hidden), (weight_hbm, weight)))
            ]
        )
    for copy in small + [copy for pair in large for copy in pair] + later:
        copy.start()
    for copy in small:
        copy.wait()
    cells = noisy[...].astype(F32)
    rows[...] = jnp.concatenate(
        [cells[f, :, w, :] for f in range(cells.shape[0]) for w in range(cells.shape[2])], axis=0
    ).T.astype(BF16)
    sums, first, second = 0.0, 0.0, 0.0
    row = lax.broadcasted_iota(jnp.int32, (16, wide), 0)
    for part in range(parts):
        for copy in large[part]:
            copy.wait()
        cut = slice(part * wide, (part + 1) * wide)
        x = hidden[:, cut].astype(F32)
        embed = time_embed[:, cut]
        scale = 1.0 + (modulation[1:2, cut] + embed)
        shift = modulation[0:1, cut] + embed
        scaled = x * scale
        high = scaled.astype(BF16)
        low = (scaled - high.astype(F32)).astype(BF16)
        scale_high = scale.astype(BF16).astype(F32)
        shift_high = shift.astype(BF16).astype(F32)
        extra = jnp.where(row == 0, scale_high, 0.0)
        extra = jnp.where(row == 1, scale - scale_high, extra)
        extra = jnp.where(row == 2, shift_high, extra)
        extra = jnp.where(row == 3, shift - shift_high, extra).astype(BF16)
        stacked = jnp.concatenate([high, low, extra], axis=0)
        sums = sums + lax.dot_general(
            stacked, weight[:, cut], (((1,), (1,)), ((), ())), preferred_element_type=F32
        )
        first = first + jnp.sum(x, axis=1, keepdims=True)
        second = second + jnp.sum(x * x, axis=1, keepdims=True)
    out[0:tokens, 0:outs] = sums[0:tokens] + sums[tokens : 2 * tokens]
    lane = lax.broadcasted_iota(jnp.int32, (tokens, outs), 1)
    out[0:tokens, outs : 2 * outs] = jnp.where(lane == 0, first, second)
    base = 2 * tokens
    out[tokens : tokens + 1, 0:outs] = sums[base : base + 1] + sums[base + 1 : base + 2]
    out[tokens : tokens + 1, outs : 2 * outs] = sums[base + 2 : base + 3] + sums[base + 3 : base + 4]
    out[tokens + 1 :, :] = jnp.zeros((out.shape[0] - tokens - 1, out.shape[1]), F32)
    for copy in later:
        copy.wait()


def stage_kernel(_, step, weight_hbm, bias_hbm, *refs):
    bias, arrived, refs = refs[-2], refs[-1], refs[:-2]
    count = (len(refs) - 3) // 2
    step_row, weight, turned = refs[count : count + 3]
    taps = weight_hbm.shape[0]
    pairs = [(weight_hbm, weight.at[0:taps]), (bias_hbm, bias)]
    pairs += list(zip(refs[:count], refs[count + 3 :], strict=True))
    copies = [
        pltpu.make_async_copy(source, target, arrived.at[i])
        for i, (source, target) in enumerate(pairs)
    ]
    for copy in copies:
        copy.start()
    step_row[...] = jnp.full(step_row.shape, step[0], F32)
    copies[1].wait()
    rest, below = bias[...], weight.shape[0] - taps
    row = lax.broadcasted_iota(jnp.int32, (below, rest.shape[1]), 0)
    rows = jnp.zeros(row.shape, F32)
    for part in range(3):
        piece = rest.astype(BF16).astype(F32)
        rows = jnp.where(row == part, piece, rows)
        rest = rest - piece
    weight[taps:] = rows.astype(BF16)
    copies[0].wait()
    turned[...] = weight[...].T
    for copy in copies[2:]:
        copy.wait()


def message_kernel(mine, other, bias, place, noisy, out, *, features, cells, channels):
    tokens, outs = place.shape[0], bias.shape[1]
    total = mine[...] + other[...]
    average = total[0:tokens, outs : outs + 1] / features
    variance = total[0:tokens, outs + 1 : outs + 2] / features - average * average
    inverse = lax.rsqrt(variance + 1e-06)
    scale_sum = total[tokens : tokens + 1, 0:outs]
    shift_sum = total[tokens : tokens + 1, outs : 2 * outs]
    velocity = inverse * (total[0:tokens, 0:outs] - average * scale_sum) + (shift_sum + bias[...])
    velocity = velocity.astype(BF16)
    spread = lax.dot_general(
        velocity, place[...], (((0,), (0,)), ((), ())), preferred_element_type=F32
    )
    field = spread[0:channels, 0:cells]
    for part in range(1, outs // channels):
        field = field + spread[
            part * channels : (part + 1) * channels, part * cells : (part + 1) * cells
        ]
    for target in range(out.shape[0]):
        out[target, :, 0:cells] = field.astype(BF16)
        out[target, :, cells:] = noisy[...]


def latents(messages, first, step, std, mean, sections, members, cells):
    lat = std.shape[1]
    diagonal = lax.broadcasted_iota(jnp.int32, (lat, lat), 0) == lax.broadcasted_iota(
        jnp.int32, (lat, lat), 1
    )
    deviation = jnp.sum(jnp.where(diagonal, std[...], 0.0), axis=1, keepdims=True)
    middle = jnp.sum(jnp.where(diagonal, mean[...], 0.0), axis=1, keepdims=True)
    parts = [messages[first + s * members].astype(F32) for s in range(sections)]
    tile = cells // sections
    frames = []
    for frame in range(sections):
        cut = slice(cells + frame * tile, cells + (frame + 1) * tile)
        noisy = jnp.concatenate([part[:, cut] for part in parts], axis=1)
        latent = (noisy - step * parts[frame][:, 0:cells]) * deviation + middle
        frames.append(latent.astype(BF16).astype(F32))
    return jnp.concatenate(frames, axis=1)


def conv_frames(normed, conv, first_column, columns, frames, a, totals):
    height, deep = normed.shape[3:]
    half = conv.shape[2]
    size = frames * columns * height
    for i, first in enumerate(range(9 * a, 9 * a + 9, 2)):
        group = range(first, min(first + 2, 9 * a + 9))
        window = jnp.concatenate(
            [
                normed[t // 3 % 3, a : a + frames, pl.ds(first_column + t % 3, columns)].reshape(
                    size, deep
                )
                for t in group
            ],
            axis=1,
        )
        weight = conv[first : first + len(group)].reshape(len(group) * deep, half)
        which = (a + i) % 2
        totals[which] = totals[which] + jnp.dot(window, weight, preferred_element_type=F32)


def conv_tile(normed, conv, first_column, columns, frames):
    totals = [0.0, 0.0]
    for a in range(3):
        conv_frames(normed, conv, first_column, columns, frames, a, totals)
    return totals[0] + totals[1]


def norm_kernel(
    step, messages, std, mean, weight_mine, weight_other, gain, conv,
    partial, normed, rolled, *, frames, height, width, k, sections, members
):
    mine, side, member = (lax.axis_index(axis) for axis in ("section", "tp", "sp"))
    first_frame = member * frames - 2
    cells = height * width
    lat = messages.shape[1]
    lanes = 2 * frames * cells
    half = weight_mine.shape[0]
    deep = gain.shape[2]
    columns = width // sections
    per_half = half // deep
    block = jnp.where((mine // per_half) == side, 0, per_half) + mine % per_half
    rest = (step[:, 0:1], std, mean, sections, members, cells)
    earlier = latents(messages, jnp.maximum(member - 1, 0), *rest)
    earlier = jnp.where(member > 0, earlier, 0.0)
    x = jnp.concatenate([earlier, latents(messages, member, *rest)], axis=1)
    position = lax.broadcasted_iota(jnp.int32, (1, lanes), 1)
    at_row = position % height
    at_column = (position // height) % width
    for b in range(3):
        for e in range(3):
            offset = (e - 1) * height + (b - 1)
            moved = x if offset == 0 else pltpu.roll(x, (-offset) % lanes, axis=1)
            row, column = at_row + (b - 1), at_column + (e - 1)
            inside = (row >= 0) & (row < height) & (column >= 0) & (column < width)
            moved = jnp.where(inside, moved, 0.0)
            first = (3 * b + e) * lat
            rolled[first : first + lat, :] = moved.astype(BF16)
    half_gain = 0.5 * gain[mine]
    edge = lax.broadcasted_iota(jnp.int32, (cells, 1), 0) % height
    zero_column = jnp.zeros((height, deep), BF16)
    totals = [0.0, 0.0]
    for frame in range(frames + 2):
        stacked = windows(rolled, frame, cells, weight_mine.shape[1])
        squares, halves = 0.0, []
        for weight in (weight_mine, weight_other):
            product = jnp.dot(weight[...], stacked, preferred_element_type=F32)
            squares = squares + jnp.sum(product * product, axis=0, keepdims=True)
            halves.append(product)
        inverse = lax.rsqrt(squares / (2 * half) + 1e-06)
        chosen = jnp.where(block < per_half, halves[0], halves[1])
        value = chosen[0:deep]
        for i in range(1, per_half):
            value = jnp.where(block % per_half == i, chosen[i * deep : (i + 1) * deep], value)
        value = (value.astype(BF16).astype(F32) * inverse).T * half_gain
        value = value * (1.0 + jnp.tanh(value))
        if frame < 2:
            value = jnp.where(first_frame + frame >= 0, value, 0.0)
        above = jnp.where(edge == 0, 0.0, pltpu.roll(value, 1, axis=0))
        below = jnp.where(edge == height - 1, 0.0, pltpu.roll(value, cells - 1, axis=0))
        for b, shifted in enumerate((above, value, below)):
            normed[b, frame, 1 : width + 1] = shifted.astype(BF16).reshape(width, height, deep)
            normed[b, frame, 0] = zero_column
            normed[b, frame, width + 1] = zero_column
        if frame >= frames - 1:
            first = (mine ^ k) * columns
            conv_frames(normed, conv, first, columns, frames, frame + 1 - frames, totals)
    partial[...] = (totals[0] + totals[1]).astype(BF16)


def tile_kernel(normed, conv, partial, *, columns, frames, k):
    partial[...] = conv_tile(normed, conv, (lax.axis_index("section") ^ k) * columns, columns, frames).astype(
        partial.dtype
    )


def windows(rolled, frame, cells, depth):
    pieces = [rolled[:, (frame + a) * cells : (frame + a + 1) * cells] for a in range(3)]
    rest = depth - 3 * rolled.shape[0]
    return jnp.concatenate(pieces + [jnp.ones((rest, cells), BF16)], axis=0)


def own_kernel(normed, conv, rolled, weight, bias, total, own, *, columns, frames, cells):
    mine = lax.axis_index("section")
    height = normed.shape[3]
    size = columns * height
    for frame in range(frames):
        product = lax.dot_general(
            windows(rolled, frame + 2, cells, weight.shape[0]), weight[...],
            (((0,), (0,)), ((), ())), preferred_element_type=F32,
        )
        own[frame] = product.astype(BF16)
    sums = conv_tile(normed, conv, mine * columns, columns, frames)
    rows = pl.ds(pl.multiple_of(mine * size, size), size)
    for frame in range(frames):
        cut = slice(frame * size, (frame + 1) * size)
        total[cut, :] = sums[cut] + own[frame, rows, :].astype(F32) + bias[...]


def finish_kernel(order, first, *refs):
    parts, out = refs[:-1], refs[-1]
    frames, height, columns = out.shape[:3]
    rows = height * columns
    for frame in range(frames):
        cut = slice(frame * rows, (frame + 1) * rows)
        total = first[cut, :]
        for part in parts:
            total = total + part[cut, :].astype(F32)
        placed = jnp.dot(order[...], total.astype(BF16), preferred_element_type=F32)
        out[frame] = placed.reshape(height, columns, -1).astype(BF16)


def vmem(count):
    return [pl.BlockSpec(memory_space=pltpu.VMEM)] * count


SMEM = pl.BlockSpec(memory_space=pltpu.SMEM)
HBM = pl.BlockSpec(memory_space=pltpu.HBM)


VMEM_LIMIT = 12 * 2**20


def call(kernel, shapes, in_specs, scratch=(), last=False):
    single = not isinstance(shapes, (list, tuple))
    specs = pl.BlockSpec(memory_space=pltpu.VMEM) if single else vmem(len(shapes))
    if not last:
        local = [pltpu.VMEM(s.shape, s.dtype) for s in ([shapes] if single else shapes)]
        shapes = local[0] if single else local
    run = pl.pallas_call(
        kernel, out_shape=shapes, in_specs=in_specs, out_specs=specs, scratch_shapes=list(scratch),
        compiler_params=pltpu.CompilerParams(vmem_limit_bytes=VMEM_LIMIT),
    )

    def constrained(*args):
        return run(
            *[
                arg if spec is SMEM else pltpu.with_memory_space_constraint(arg, spec.memory_space)
                for arg, spec in zip(args, in_specs, strict=True)
            ]
        )

    return constrained


def deep_rows(weight):
    return (weight.shape[0] + 3 + 127) // 128 * 128


def staged(after, step, weight, bias, *arrays):
    shapes = [
        jax.ShapeDtypeStruct((1, 128), F32),
        jax.ShapeDtypeStruct((deep_rows(weight), weight.shape[1]), weight.dtype),
        jax.ShapeDtypeStruct((weight.shape[1], deep_rows(weight)), weight.dtype),
    ]
    shapes += [jax.ShapeDtypeStruct(x.shape, x.dtype) for x in arrays]
    return call(
        stage_kernel, shapes, vmem(1) + [SMEM] + [HBM] * (2 + len(arrays)),
        [pltpu.VMEM(bias.shape, F32), pltpu.SemaphoreType.DMA((2 + len(arrays),))],
    )(after, step, weight, bias, *arrays)


def token_places(height, width):
    cells = height * width
    table = np.zeros((cells // 4, 4, cells), np.float32)
    for i in range(height // 2):
        for j in range(width // 2):
            for p in range(2):
                for q in range(2):
                    cell = (2 * j + q) * height + 2 * i + p
                    table[i * (width // 2) + j, 2 * p + q, cell] = 1.0
    return table.reshape(cells // 4, 4 * cells)


def row_order(height, columns):
    table = np.zeros((height * columns, height * columns), np.float32)
    for h in range(height):
        for w in range(columns):
            table[h * columns + w, w * height + h] = 1.0
    return table


def send_order(sections):
    order = list(range(1, sections))
    return sorted(order, key=lambda k: (k == sections - 1, -k))


def sectioned_shards(
    hidden, modulation, time_embed, head_weight, head_bias, noisy, step_size,
    latent_mean, latent_std, in_weight, in_bias, norm_gain, conv_weight, conv_bias,
):
    frames, height, columns, lat = noisy.shape
    sections, halves = lax.axis_size("section"), lax.axis_size("tp")
    members = lax.axis_size("sp")
    width, half = columns * sections, in_weight.shape[2]
    cells = height * width
    tokens, local = hidden.shape
    outs = head_weight.shape[1]
    deep = conv_weight.shape[1]
    swap = [(i, i ^ 1) for i in range(halves)]
    taps = in_weight.shape[0]

    parts = 1
    head_in = (
        hidden, modulation, time_embed.reshape(1, local), head_weight.T, noisy,
    )
    kept = (jnp.asarray(token_places(height, width), BF16), head_bias.reshape(1, outs))
    sums, noisy_rows, place, head_bias = call(
        lambda *refs: head_kernel(*refs, parts=parts),
        [
            jax.ShapeDtypeStruct((tokens + 8, 2 * outs), F32),
            jax.ShapeDtypeStruct((lat, frames * columns * height), BF16),
        ]
        + [jax.ShapeDtypeStruct(x.shape, x.dtype) for x in kept],
        [HBM] * (len(head_in) + len(kept)),
        [pltpu.VMEM(x.shape, x.dtype) for x in head_in]
        + [pltpu.SemaphoreType.DMA((5 + 2 * parts,))],
    )(*head_in, *kept)
    sums_other = lax.ppermute(sums, "tp", swap)
    message = call(
        lambda *refs: message_kernel(
            *refs, features=local * halves, cells=cells, channels=lat
        ),
        jax.ShapeDtypeStruct((sections * members, lat, 2 * cells), BF16), vmem(5),
    )(sums, sums_other, head_bias, place, noisy_rows)
    messages = lax.all_to_all(message, ("section", "sp"), 0, 0)
    step, weight, weight_mine, latent_std, latent_mean, conv, gain, order, conv_bias = staged(
        message, step_size, in_weight.reshape(taps * lat, half), in_bias.reshape(1, half),
        latent_std.reshape(1, lat), latent_mean.reshape(1, lat), conv_weight,
        norm_gain.reshape(sections, 1, deep), jnp.asarray(row_order(height, columns), BF16),
        conv_bias.reshape(1, half),
    )
    weight_other = lax.ppermute(weight_mine, "tp", swap)

    size = frames * columns * height
    sends = send_order(sections)
    partials = {}
    partials[sends[0]], normed, rolled = call(
        lambda *refs: norm_kernel(
            *refs, frames=frames, height=height, width=width, k=sends[0],
            sections=sections, members=members
        ),
        [
            jax.ShapeDtypeStruct((size, half), BF16),
            jax.ShapeDtypeStruct((3, frames + 2, width + 2, height, deep), BF16),
            jax.ShapeDtypeStruct((9 * lat, 2 * frames * cells), BF16),
        ],
        vmem(8),
    )(step, messages, latent_std, latent_mean, weight_mine, weight_other, gain, conv)
    received = {}
    for k in sends:
        if k not in partials:
            partials[k] = call(
                lambda *refs: tile_kernel(*refs, columns=columns, frames=frames, k=k),
                jax.ShapeDtypeStruct((size, half), BF16), vmem(2),
            )(normed, conv)
        received[k] = lax.ppermute(partials[k], "section", [(i, i ^ k) for i in range(sections)])
    total = call(
        lambda *refs: own_kernel(*refs, columns=columns, frames=frames, cells=cells),
        jax.ShapeDtypeStruct((size, half), F32), vmem(5),
        [pltpu.VMEM((frames, cells, half), BF16)],
    )(normed, conv, rolled, weight, conv_bias)
    return call(
        finish_kernel, jax.ShapeDtypeStruct((frames, height, columns, half), BF16),
        vmem(1 + sections), last=True,
    )(order, total, *[received[k] for k in sends])


def sectioned(mesh):
    def fits(hidden, head_weight, noisy, in_weight, conv_weight):
        frames, height, columns, _ = noisy.shape
        sections = mesh.shape["section"]
        cells = height * columns * sections
        deep = conv_weight.shape[1]
        return (
            sections == frames
            and sections & (sections - 1) == 0
            and hidden.shape[0] * 4 == cells
            and mesh.shape["tp"] == 2
            and in_weight.shape[2] == 2 * deep
            and 2 * in_weight.shape[2] == sections * deep
            and deep % 128 == 0
            and 2 * head_weight.shape[1] == deep
            and height % 16 == 0
            and cells % 128 == 0
        )

    return fits


def solution(mesh):
    placed = (
        P(("groups", "sp", "section"), "tp"),
        P(None, "tp"),
        P(("groups", "tp")),
        P("tp", None),
        P(),
        P(("groups", "sp"), None, "section", None),
        P("groups"),
        P(),
        P(),
        P(None, None, "tp"),
        P("tp"),
        P(),
        P(None, "section", "tp"),
        P("tp"),
    )
    fits = sectioned(mesh)

    def shards(*args):
        if not fits(args[0], args[3], args[5], args[9], args[12]):
            return general_shards(*args)
        return sectioned_shards(*args)

    return jax.shard_map(
        shards,
        mesh=mesh,
        in_specs=placed,
        out_specs=P(("groups", "sp"), None, "section", "tp"),
        check_vma=False,
    )
```

```python
import jax
import jax.numpy as jnp
import numpy as np
from jax import lax
from jax.experimental import pallas as pl
from jax.experimental.pallas import tpu as pltpu
from jax.sharding import PartitionSpec as P

F32 = jnp.float32
BF16 = jnp.bfloat16


def padded_2(value, sides, width):
    for axis, dim in sides:
        count, length = (lax.axis_size(axis), value.shape[dim])
        up = [(i, (i + 1) % count) for i in range(count - 1)]
        down = [(j, i) for i, j in up]
        last = lax.slice_in_dim(value, length - width, length, axis=dim)
        leading = lax.slice_in_dim(value, 0, width, axis=dim)
        before = lax.ppermute(last, axis, up)
        after = lax.ppermute(leading, axis, down)
        value = jnp.concatenate([before, value, after], axis=dim)
    return value


def passed_along(value, axis, by):
    count = lax.axis_size(axis)
    pairs = [(i, i + by) for i in range(count) if 0 <= i + by < count]
    return lax.ppermute(value, axis, pairs)


def conv_taps(padded, weight, frames, height, columns):
    channels = padded.shape[3]
    result = jnp.zeros((frames * height * columns, weight.shape[2]), jnp.float32)
    for offset_time in range(3):
        for offset_row in range(3):
            slab = padded[offset_time : offset_time + frames, offset_row : offset_row + height]
            window = jnp.concatenate(
                [slab[:, :, 0:columns], slab[:, :, 1 : columns + 1], slab[:, :, 2 : columns + 2]],
                axis=3,
            )
            first = 9 * offset_time + 3 * offset_row
            taps = weight[first : first + 3].reshape(3 * channels, weight.shape[2])
            result = result + jnp.dot(
                window.reshape(-1, 3 * channels), taps, preferred_element_type=jnp.float32
            )
    return result


def activate(source, gain_vector):
    values = source.astype(jnp.float32)
    squares = jnp.mean(values * values, axis=-1, keepdims=True)
    return jax.nn.silu(values * lax.rsqrt(squares + 1e-06) * gain_vector).astype(jnp.bfloat16)


def pad_rows(source):
    return jnp.pad(source, ((0, 0), (1, 1), (0, 0), (0, 0)))


def general_shards(
    hidden, modulation, time_embed, head_weight, head_bias, noisy, step_size,
    latent_mean, latent_std, in_weight, in_bias, norm_gain, conv_weight, conv_bias,
):
    frames, height, columns, lat_channels = noisy.shape
    sections = lax.axis_size("section")
    half_channels = in_weight.shape[2]
    features = hidden.shape[1] * lax.axis_size("tp")
    values = hidden.astype(jnp.float32)
    row_sums, square_sums = lax.psum(
        (jnp.sum(values, axis=1), jnp.sum(values * values, axis=1)), "tp"
    )
    average = row_sums / features
    variance = square_sums / features - average * average
    shift_term = modulation[0] + time_embed
    scale_term = modulation[1] + time_embed
    modulated = (
        (values - average[:, None]) * lax.rsqrt(variance[:, None] + 1e-06) * (1.0 + scale_term)
        + shift_term
    ).astype(jnp.bfloat16)
    partial_sum = jnp.dot(modulated, head_weight, preferred_element_type=jnp.float32)
    velocity = (lax.psum(partial_sum, "tp") + head_bias).astype(jnp.bfloat16)
    band_rows = velocity.shape[0] * 2 // (columns * sections)
    outgoing = velocity.reshape(band_rows, sections, -1)
    arrived = lax.all_to_all(outgoing, "section", split_axis=1, concat_axis=0, tiled=True)
    latent_field = arrived.reshape(frames, height // 2, columns // 2, 2, 2, lat_channels)
    latent_field = jnp.transpose(latent_field, (0, 1, 3, 2, 4, 5)).reshape(
        frames, height, columns, lat_channels
    )
    latent = (
        (noisy.astype(jnp.float32) - step_size[0] * latent_field.astype(jnp.float32)) * latent_std
        + latent_mean
    ).astype(jnp.bfloat16)
    latent_wide = padded_2(latent, (("section", 2),), 2)
    earlier = passed_along(latent_wide, "sp", 1)
    stacked = pad_rows(jnp.concatenate([earlier, latent_wide], axis=0))
    extended = (conv_taps(stacked, in_weight, frames + 2, height, columns + 2) + in_bias).astype(
        jnp.bfloat16
    )
    extended = extended.reshape(frames + 2, height, columns + 2, half_channels)
    upblock_half = extended[2:, :, 1 : columns + 1]
    extended_full = lax.all_gather(extended, "tp", axis=3, tiled=True)
    normed = activate(extended_full, norm_gain)
    frame_index = lax.axis_index("sp") * frames - 2 + jnp.arange(frames + 2, dtype=jnp.int32)
    column_index = (
        lax.axis_index("section") * columns - 1 + jnp.arange(columns + 2, dtype=jnp.int32)
    )
    inside_cols = (column_index >= 0) & (column_index < columns * sections)
    inside = (frame_index >= 0)[:, None, None, None] & inside_cols[None, None, :, None]
    conv_input = pad_rows(jnp.where(inside, normed, jnp.zeros_like(normed)))
    full_weight = lax.all_gather(conv_weight, "section", axis=1, tiled=True)
    mixed = conv_taps(conv_input, full_weight, frames, height, columns)
    decoded = (
        upblock_half.astype(jnp.float32).reshape(-1, half_channels) + mixed + conv_bias
    ).astype(jnp.bfloat16)
    return decoded.reshape(frames, height, columns, half_channels)


def head_kernel(
    hidden_hbm, modulation_hbm, embed_hbm, weight_hbm, noisy_hbm, place_hbm, bias_hbm,
    out, rows, place, bias, hidden, modulation, time_embed, weight, noisy, arrived, *, parts
):
    tokens, features = hidden.shape
    outs = weight.shape[0]
    wide = features // parts
    small = [
        pltpu.make_async_copy(source, target, arrived.at[i])
        for i, (source, target) in enumerate(
            ((noisy_hbm, noisy), (modulation_hbm, modulation), (embed_hbm, time_embed))
        )
    ]
    later = [
        pltpu.make_async_copy(source, target, arrived.at[3 + 2 * parts + i])
        for i, (source, target) in enumerate(((place_hbm, place), (bias_hbm, bias)))
    ]
    large = []
    for part in range(parts):
        cut = pl.ds(part * wide, wide)
        large.append(
            [
                pltpu.make_async_copy(
                    source.at[:, cut], target.at[:, cut], arrived.at[3 + 2 * part + i]
                )
                for i, (source, target) in enumerate(((hidden_hbm, hidden), (weight_hbm, weight)))
            ]
        )
    for copy in small + [copy for pair in large for copy in pair] + later:
        copy.start()
    for copy in small:
        copy.wait()
    cells = noisy[...].astype(F32)
    rows[...] = jnp.concatenate(
        [cells[f, :, w, :] for f in range(cells.shape[0]) for w in range(cells.shape[2])], axis=0
    ).T.astype(BF16)
    sums, first, second = 0.0, 0.0, 0.0
    row = lax.broadcasted_iota(jnp.int32, (16, wide), 0)
    for part in range(parts):
        for copy in large[part]:
            copy.wait()
        cut = slice(part * wide, (part + 1) * wide)
        x = hidden[:, cut].astype(F32)
        embed = time_embed[:, cut]
        scale = 1.0 + (modulation[1:2, cut] + embed)
        shift = modulation[0:1, cut] + embed
        scaled = x * scale
        high = scaled.astype(BF16)
        low = (scaled - high.astype(F32)).astype(BF16)
        scale_high = scale.astype(BF16).astype(F32)
        shift_high = shift.astype(BF16).astype(F32)
        extra = jnp.where(row == 0, scale_high, 0.0)
        extra = jnp.where(row == 1, scale - scale_high, extra)
        extra = jnp.where(row == 2, shift_high, extra)
        extra = jnp.where(row == 3, shift - shift_high, extra).astype(BF16)
        over = (((1,), (1,)), ((), ()))
        main = lax.dot_general(high, weight[:, cut], over, preferred_element_type=F32)
        rest = lax.dot_general(
            jnp.concatenate([low, extra], axis=0), weight[:, cut], over, preferred_element_type=F32
        )
        sums = sums + jnp.concatenate([main, rest], axis=0)
        first = first + jnp.sum(x, axis=1, keepdims=True)
        second = second + jnp.sum(x * x, axis=1, keepdims=True)
    out[0:tokens, 0:outs] = sums[0:tokens] + sums[tokens : 2 * tokens]
    lane = lax.broadcasted_iota(jnp.int32, (tokens, outs), 1)
    out[0:tokens, outs : 2 * outs] = jnp.where(lane == 0, first, second)
    base = 2 * tokens
    out[tokens : tokens + 1, 0:outs] = sums[base : base + 1] + sums[base + 1 : base + 2]
    out[tokens : tokens + 1, outs : 2 * outs] = sums[base + 2 : base + 3] + sums[base + 3 : base + 4]
    out[tokens + 1 :, :] = jnp.zeros((out.shape[0] - tokens - 1, out.shape[1]), F32)
    for copy in later:
        copy.wait()


def stage_kernel(_, step, weight_hbm, bias_hbm, *refs):
    bias, arrived, refs = refs[-2], refs[-1], refs[:-2]
    count = (len(refs) - 3) // 2
    step_row, weight, turned = refs[count : count + 3]
    taps = weight_hbm.shape[0]
    pairs = [(weight_hbm, weight.at[0:taps]), (bias_hbm, bias)]
    pairs += list(zip(refs[:count], refs[count + 3 :], strict=True))
    copies = [
        pltpu.make_async_copy(source, target, arrived.at[i])
        for i, (source, target) in enumerate(pairs)
    ]
    for copy in copies:
        copy.start()
    step_row[...] = jnp.full(step_row.shape, step[0], F32)
    copies[1].wait()
    rest, below = bias[...], weight.shape[0] - taps
    row = lax.broadcasted_iota(jnp.int32, (below, rest.shape[1]), 0)
    rows = jnp.zeros(row.shape, F32)
    for part in range(3):
        piece = rest.astype(BF16).astype(F32)
        rows = jnp.where(row == part, piece, rows)
        rest = rest - piece
    weight[taps:] = rows.astype(BF16)
    copies[0].wait()
    turned[...] = weight[...].T
    for copy in copies[2:]:
        copy.wait()


def message_kernel(mine, other, bias, place, noisy, out, *, features, cells, channels):
    tokens, outs = place.shape[0], bias.shape[1]
    total = mine[...] + other[...]
    average = total[0:tokens, outs : outs + 1] / features
    variance = total[0:tokens, outs + 1 : outs + 2] / features - average * average
    inverse = lax.rsqrt(variance + 1e-06)
    scale_sum = total[tokens : tokens + 1, 0:outs]
    shift_sum = total[tokens : tokens + 1, outs : 2 * outs]
    velocity = inverse * (total[0:tokens, 0:outs] - average * scale_sum) + (shift_sum + bias[...])
    velocity = velocity.astype(BF16)
    spread = lax.dot_general(
        velocity, place[...], (((0,), (0,)), ((), ())), preferred_element_type=F32
    )
    field = spread[0:channels, 0:cells]
    for part in range(1, outs // channels):
        field = field + spread[
            part * channels : (part + 1) * channels, part * cells : (part + 1) * cells
        ]
    for target in range(out.shape[0]):
        out[target, :, 0:cells] = field.astype(BF16)
        out[target, :, cells:] = noisy[...]


def latents(messages, first, step, std, mean, sections, members, cells):
    lat = std.shape[1]
    diagonal = lax.broadcasted_iota(jnp.int32, (lat, lat), 0) == lax.broadcasted_iota(
        jnp.int32, (lat, lat), 1
    )
    deviation = jnp.sum(jnp.where(diagonal, std[...], 0.0), axis=1, keepdims=True)
    middle = jnp.sum(jnp.where(diagonal, mean[...], 0.0), axis=1, keepdims=True)
    parts = [messages[first + s * members].astype(F32) for s in range(sections)]
    tile = cells // sections
    frames = []
    for frame in range(sections):
        cut = slice(cells + frame * tile, cells + (frame + 1) * tile)
        noisy = jnp.concatenate([part[:, cut] for part in parts], axis=1)
        latent = (noisy - step * parts[frame][:, 0:cells]) * deviation + middle
        frames.append(latent.astype(BF16).astype(F32))
    return jnp.concatenate(frames, axis=1)


def digit(value, base, count):
    if base & (base - 1) == 0 and count & (count - 1) == 0:
        return (value >> (base.bit_length() - 1)) & (count - 1)
    return value // base % count


def conv_frames(normed, conv, first_column, columns, frames, a, totals):
    height, deep = normed.shape[3:]
    half = conv.shape[2]
    size = frames * columns * height
    for i, first in enumerate(range(9 * a, 9 * a + 9, 2)):
        group = range(first, min(first + 2, 9 * a + 9))
        window = jnp.concatenate(
            [
                normed[t // 3 % 3, a : a + frames, pl.ds(first_column + t % 3, columns)].reshape(
                    size, deep
                )
                for t in group
            ],
            axis=1,
        )
        weight = conv[first : first + len(group)].reshape(len(group) * deep, half)
        which = (a + i) % 2
        totals[which] = totals[which] + jnp.dot(window, weight, preferred_element_type=F32)


def conv_tile(normed, conv, first_column, columns, frames):
    totals = [0.0, 0.0]
    for a in range(3):
        conv_frames(normed, conv, first_column, columns, frames, a, totals)
    return totals[0] + totals[1]


def norm_kernel(
    step, messages, std, mean, weight_mine, weight_other, gain, conv,
    partial, normed, rolled, *, frames, height, width, k, sections, members
):
    mine, side, member = (lax.axis_index(axis) for axis in ("section", "tp", "sp"))
    first_frame = member * frames - 2
    cells = height * width
    lat = messages.shape[1]
    lanes = 2 * frames * cells
    half = weight_mine.shape[0]
    deep = gain.shape[2]
    columns = width // sections
    per_half = half // deep
    block = jnp.where((mine // per_half) == side, 0, per_half) + mine % per_half
    rest = (step[:, 0:1], std, mean, sections, members, cells)
    earlier = latents(messages, jnp.maximum(member - 1, 0), *rest)
    earlier = jnp.where(member > 0, earlier, 0.0)
    x = jnp.concatenate([earlier, latents(messages, member, *rest)], axis=1)
    position = lax.broadcasted_iota(jnp.int32, (1, lanes), 1)
    at_row, at_column = digit(position, 1, height), digit(position, height, width)
    in_row = {0: at_row > 0, 2: at_row < height - 1}
    in_column = {0: at_column > 0, 2: at_column < width - 1}
    for b in range(3):
        for e in range(3):
            offset = (e - 1) * height + (b - 1)
            moved = x if offset == 0 else pltpu.roll(x, (-offset) % lanes, axis=1)
            masks = [kind[i] for kind, i in ((in_row, b), (in_column, e)) if i != 1]
            if masks:
                moved = jnp.where(masks[0] if len(masks) == 1 else masks[0] & masks[1], moved, 0.0)
            first = (3 * b + e) * lat
            rolled[first : first + lat, :] = moved.astype(BF16)
    half_gain = 0.5 * gain[mine]
    edge = digit(lax.broadcasted_iota(jnp.int32, (cells, 1), 0), 1, height)
    zero_column = jnp.zeros((height, deep), BF16)
    totals = [0.0, 0.0]
    for frame in range(frames + 2):
        stacked = windows(rolled, frame, cells, weight_mine.shape[1])
        squares, halves = 0.0, []
        for weight in (weight_mine, weight_other):
            product = jnp.dot(weight[...], stacked, preferred_element_type=F32)
            squares = squares + jnp.sum(product * product, axis=0, keepdims=True)
            halves.append(product)
        inverse = lax.rsqrt(squares / (2 * half) + 1e-06)
        chosen = jnp.where(block < per_half, halves[0], halves[1])
        value = chosen[0:deep]
        for i in range(1, per_half):
            value = jnp.where(block % per_half == i, chosen[i * deep : (i + 1) * deep], value)
        value = (value.astype(BF16).astype(F32) * inverse).T * half_gain
        value = value * (1.0 + jnp.tanh(value))
        if frame < 2:
            value = jnp.where(first_frame + frame >= 0, value, 0.0)
        above = jnp.where(edge == 0, 0.0, pltpu.roll(value, 1, axis=0))
        below = jnp.where(edge == height - 1, 0.0, pltpu.roll(value, cells - 1, axis=0))
        for b, shifted in enumerate((above, value, below)):
            normed[b, frame, 1 : width + 1] = shifted.astype(BF16).reshape(width, height, deep)
            normed[b, frame, 0] = zero_column
            normed[b, frame, width + 1] = zero_column
        if frame >= frames - 1:
            first = (mine ^ k) * columns
            conv_frames(normed, conv, first, columns, frames, frame + 1 - frames, totals)
    partial[...] = (totals[0] + totals[1]).astype(BF16)


def tile_kernel(normed, conv, partial, *, columns, frames, k):
    partial[...] = conv_tile(normed, conv, (lax.axis_index("section") ^ k) * columns, columns, frames).astype(
        partial.dtype
    )


def windows(rolled, frame, cells, depth):
    pieces = [rolled[:, (frame + a) * cells : (frame + a + 1) * cells] for a in range(3)]
    rest = depth - 3 * rolled.shape[0]
    return jnp.concatenate(pieces + [jnp.ones((rest, cells), BF16)], axis=0)


def own_kernel(normed, conv, rolled, weight, bias, total, own, *, columns, frames, cells):
    mine = lax.axis_index("section")
    height = normed.shape[3]
    size = columns * height
    for frame in range(frames):
        product = lax.dot_general(
            windows(rolled, frame + 2, cells, weight.shape[0]), weight[...],
            (((0,), (0,)), ((), ())), preferred_element_type=F32,
        )
        own[frame] = product.astype(BF16)
    sums = conv_tile(normed, conv, mine * columns, columns, frames)
    rows = pl.ds(pl.multiple_of(mine * size, size), size)
    for frame in range(frames):
        cut = slice(frame * size, (frame + 1) * size)
        total[cut, :] = sums[cut] + own[frame, rows, :].astype(F32) + bias[...]


def finish_kernel(order, first, *refs):
    parts, out = refs[:-1], refs[-1]
    frames, height, columns = out.shape[:3]
    rows = height * columns
    for frame in range(frames):
        cut = slice(frame * rows, (frame + 1) * rows)
        total = first[cut, :]
        for part in parts:
            total = total + part[cut, :].astype(F32)
        placed = jnp.dot(order[...], total.astype(BF16), preferred_element_type=F32)
        out[frame] = placed.reshape(height, columns, -1).astype(BF16)


def vmem(count):
    return [pl.BlockSpec(memory_space=pltpu.VMEM)] * count


SMEM = pl.BlockSpec(memory_space=pltpu.SMEM)
HBM = pl.BlockSpec(memory_space=pltpu.HBM)


VMEM_LIMIT = 12 * 2**20


def call(kernel, shapes, in_specs, scratch=(), last=False):
    single = not isinstance(shapes, (list, tuple))
    specs = pl.BlockSpec(memory_space=pltpu.VMEM) if single else vmem(len(shapes))
    if not last:
        local = [pltpu.VMEM(s.shape, s.dtype) for s in ([shapes] if single else shapes)]
        shapes = local[0] if single else local
    run = pl.pallas_call(
        kernel, out_shape=shapes, in_specs=in_specs, out_specs=specs, scratch_shapes=list(scratch),
        compiler_params=pltpu.CompilerParams(vmem_limit_bytes=VMEM_LIMIT),
    )

    def constrained(*args):
        return run(
            *[
                arg if spec is SMEM else pltpu.with_memory_space_constraint(arg, spec.memory_space)
                for arg, spec in zip(args, in_specs, strict=True)
            ]
        )

    return constrained


def deep_rows(weight):
    return (weight.shape[0] + 3 + 15) // 16 * 16


def staged(after, step, weight, bias, *arrays):
    shapes = [
        jax.ShapeDtypeStruct((1, 128), F32),
        jax.ShapeDtypeStruct((deep_rows(weight), weight.shape[1]), weight.dtype),
        jax.ShapeDtypeStruct((weight.shape[1], deep_rows(weight)), weight.dtype),
    ]
    shapes += [jax.ShapeDtypeStruct(x.shape, x.dtype) for x in arrays]
    return call(
        stage_kernel, shapes, vmem(1) + [SMEM] + [HBM] * (2 + len(arrays)),
        [pltpu.VMEM(bias.shape, F32), pltpu.SemaphoreType.DMA((2 + len(arrays),))],
    )(after, step, weight, bias, *arrays)


def token_places(height, width):
    cells = height * width
    table = np.zeros((cells // 4, 4, cells), np.float32)
    for i in range(height // 2):
        for j in range(width // 2):
            for p in range(2):
                for q in range(2):
                    cell = (2 * j + q) * height + 2 * i + p
                    table[i * (width // 2) + j, 2 * p + q, cell] = 1.0
    return table.reshape(cells // 4, 4 * cells)


def row_order(height, columns):
    table = np.zeros((height * columns, height * columns), np.float32)
    for h in range(height):
        for w in range(columns):
            table[h * columns + w, w * height + h] = 1.0
    return table


def send_order(sections):
    order = list(range(1, sections))
    return sorted(order, key=lambda k: (k == sections - 1, -k))


def sectioned_shards(
    hidden, modulation, time_embed, head_weight, head_bias, noisy, step_size,
    latent_mean, latent_std, in_weight, in_bias, norm_gain, conv_weight, conv_bias,
):
    frames, height, columns, lat = noisy.shape
    sections, halves = lax.axis_size("section"), lax.axis_size("tp")
    members = lax.axis_size("sp")
    width, half = columns * sections, in_weight.shape[2]
    cells = height * width
    tokens, local = hidden.shape
    outs = head_weight.shape[1]
    deep = conv_weight.shape[1]
    swap = [(i, i ^ 1) for i in range(halves)]
    taps = in_weight.shape[0]

    parts = 1
    head_in = (
        hidden, modulation, time_embed.reshape(1, local), head_weight.T, noisy,
    )
    kept = (jnp.asarray(token_places(height, width), BF16), head_bias.reshape(1, outs))
    sums, noisy_rows, place, head_bias = call(
        lambda *refs: head_kernel(*refs, parts=parts),
        [
            jax.ShapeDtypeStruct((tokens + 8, 2 * outs), F32),
            jax.ShapeDtypeStruct((lat, frames * columns * height), BF16),
        ]
        + [jax.ShapeDtypeStruct(x.shape, x.dtype) for x in kept],
        [HBM] * (len(head_in) + len(kept)),
        [pltpu.VMEM(x.shape, x.dtype) for x in head_in]
        + [pltpu.SemaphoreType.DMA((5 + 2 * parts,))],
    )(*head_in, *kept)
    sums_other = lax.ppermute(sums, "tp", swap)
    message = call(
        lambda *refs: message_kernel(
            *refs, features=local * halves, cells=cells, channels=lat
        ),
        jax.ShapeDtypeStruct((sections * members, lat, 2 * cells), BF16), vmem(5),
    )(sums, sums_other, head_bias, place, noisy_rows)
    messages = lax.all_to_all(message, ("section", "sp"), 0, 0)
    step, weight, weight_mine, latent_std, latent_mean, conv, gain, order, conv_bias = staged(
        message, step_size, in_weight.reshape(taps * lat, half), in_bias.reshape(1, half),
        latent_std.reshape(1, lat), latent_mean.reshape(1, lat), conv_weight,
        norm_gain.reshape(sections, 1, deep), jnp.asarray(row_order(height, columns), BF16),
        conv_bias.reshape(1, half),
    )
    weight_other = lax.ppermute(weight_mine, "tp", swap)

    size = frames * columns * height
    sends = send_order(sections)
    partials = {}
    partials[sends[0]], normed, rolled = call(
        lambda *refs: norm_kernel(
            *refs, frames=frames, height=height, width=width, k=sends[0],
            sections=sections, members=members
        ),
        [
            jax.ShapeDtypeStruct((size, half), BF16),
            jax.ShapeDtypeStruct((3, frames + 2, width + 2, height, deep), BF16),
            jax.ShapeDtypeStruct((9 * lat, 2 * frames * cells), BF16),
        ],
        vmem(8),
    )(step, messages, latent_std, latent_mean, weight_mine, weight_other, gain, conv)
    received = {}
    for k in sends:
        if k not in partials:
            partials[k] = call(
                lambda *refs: tile_kernel(*refs, columns=columns, frames=frames, k=k),
                jax.ShapeDtypeStruct((size, half), BF16), vmem(2),
            )(normed, conv)
        received[k] = lax.ppermute(partials[k], "section", [(i, i ^ k) for i in range(sections)])
    total = call(
        lambda *refs: own_kernel(*refs, columns=columns, frames=frames, cells=cells),
        jax.ShapeDtypeStruct((size, half), F32), vmem(5),
        [pltpu.VMEM((frames, cells, half), BF16)],
    )(normed, conv, rolled, weight, conv_bias)
    return call(
        finish_kernel, jax.ShapeDtypeStruct((frames, height, columns, half), BF16),
        vmem(1 + sections), last=True,
    )(order, total, *[received[k] for k in sends])


def sectioned(mesh):
    def fits(hidden, head_weight, noisy, in_weight, conv_weight):
        frames, height, columns, _ = noisy.shape
        sections = mesh.shape["section"]
        cells = height * columns * sections
        deep = conv_weight.shape[1]
        return (
            sections == frames
            and sections & (sections - 1) == 0
            and hidden.shape[0] * 4 == cells
            and mesh.shape["tp"] == 2
            and in_weight.shape[2] == 2 * deep
            and 2 * in_weight.shape[2] == sections * deep
            and deep % 128 == 0
            and 2 * head_weight.shape[1] == deep
            and height % 16 == 0
            and cells % 128 == 0
        )

    return fits


def solution(mesh):
    placed = (
        P(("groups", "sp", "section"), "tp"),
        P(None, "tp"),
        P(("groups", "tp")),
        P("tp", None),
        P(),
        P(("groups", "sp"), None, "section", None),
        P("groups"),
        P(),
        P(),
        P(None, None, "tp"),
        P("tp"),
        P(),
        P(None, "section", "tp"),
        P("tp"),
    )
    fits = sectioned(mesh)

    def shards(*args):
        if not fits(args[0], args[3], args[5], args[9], args[12]):
            return general_shards(*args)
        return sectioned_shards(*args)

    return jax.shard_map(
        shards,
        mesh=mesh,
        in_specs=placed,
        out_specs=P(("groups", "sp"), None, "section", "tp"),
        check_vma=False,
    )
```
